128 devices in a mesh: grp: 2 (over core), band: 64 (over y, x, z).
Axes of the slice: x: 4, y: 4, z: 4, core: 2. Of those that a mesh axis runs over, the one named last changes fastest.
Arguments:
- fields: bfloat16 [2, 256, 640, 1280], P(None, None, ('grp', 'band')), may hold values from -4 to 4
- wave_order: int32 [640], replicated, may hold values from 0 to 639, as said below
- basis: bfloat16 [320, 2, 640, 641], P('band'), as said below
Outputs:
- whitened: bfloat16 [2, 320, 2, 641, 256], P('grp', 'band')
- factor: float32 [256, 256], replicated
The draws below stay inside these ranges and needn't reach their ends.
Inputs may be any that keep to these rules, and one draw needn't show every extreme that they name: wave_order names every wavenumber once; slots 2 k and 2 k + 1 hold m and 639 - m for some m, in either order. With a = wave_order[2 k], b = wave_order[2 k + 1], colatitude theta_i = pi (i + 1/2) / 640, mu_i = cos(theta_i) and weight_i = (pi / 640) sin(theta_i): basis[k, 0, i, j] = weight_i P(a + j, a) and basis[k, 1, i, j] = weight_i P(j - 1, b), rounded to bfloat16, where P(m, m) = exp(m log(sin theta_i) + (lgamma(m + 3/2) - lgamma(m + 1) - lgamma(3/2)) / 2), P(m + 1, m) = sqrt(2 m + 3) mu_i P(m, m), P(n, m) = sqrt((4 n^2 - 1) / (n^2 - m^2)) (mu_i P(n - 1, m) - sqrt(((n - 1)^2 - m^2) / (4 (n - 1)^2 - 1)) P(n - 2, m)), and P(n, m) = 0 for n < m or n >= 640.
All inputs are finite; a program needn't handle non-finite values.
Results may differ from the reference program's by a relative error of at most 0.012.
The reference program's roundings to bfloat16 on the way (of `fourier_table` and `spectra`) count: a program that leaves them out, or rounds other values in their place, can miss the bound.
Values may be sent and summed in bfloat16 or wider, within the bound.
No kernel may reach another device: no remote copies, remote signals or barrier semaphores. Data moves between devices by JAX's collectives and lax.ppermute only.
A program may use at most 128 MiB of HBM per device.

```python
import math
import jax
import jax.numpy as jnp
from jax import lax

NLAT = 640
NLON = 1280
LEV = 2
TIME = 256
WAVES = 640
PAIRS = 320


log_gamma_half = 0.5 * math.log(math.pi) - math.log(2.0)


def wave_slots(key):
    key_shuffle, key_side = jax.random.split(jax.random.fold_in(key, 11))
    shuffled = jax.random.permutation(key_shuffle, PAIRS).astype(jnp.int32)
    flipped = jax.random.randint(key_side, (PAIRS,), 0, 2, dtype=jnp.int32)
    mirrored = WAVES - 1 - shuffled
    first_wave = jnp.where(flipped == 1, mirrored, shuffled)
    second_wave = jnp.where(flipped == 1, shuffled, mirrored)
    return jnp.stack([first_wave, second_wave], axis=1).reshape(-1).astype(jnp.int32)


def draw_wave_order(key, part):
    return wave_slots(key)


def make_basis(first_wave, second_wave, lat_index, lat_total, wave_count):
    wave_pair = jnp.stack([first_wave, second_wave], axis=1).astype(jnp.int32)
    offset = jnp.stack([first_wave, jnp.full_like(second_wave, -1)], axis=1).astype(jnp.int32)
    colatitude = (lat_index.astype(jnp.float32) + 0.5) * (math.pi / lat_total)
    cosine = jnp.cos(colatitude)
    sine_lat = jnp.sin(colatitude)
    weight = sine_lat * (math.pi / lat_total)
    wave_grid = wave_pair[:, :, None]
    wave_float = wave_grid.astype(jnp.float32)
    diagonal_start = jnp.exp(wave_float * jnp.log(sine_lat)[None, None, :] + 0.5 * (lax.lgamma(wave_float + 1.5) - lax.lgamma(wave_float + 1.0) - log_gamma_half))

    def advance(state_pair, step_index):
        previous, before_previous = state_pair
        degree = offset[:, :, None] + step_index
        degree_float = degree.astype(jnp.float32)
        forward_coef = jnp.sqrt((4.0 * degree_float * degree_float - 1.0) / jnp.maximum(degree_float * degree_float - wave_float * wave_float, 1.0))
        lower_degree = degree_float - 1.0
        backward_coef = jnp.sqrt(jnp.maximum(lower_degree * lower_degree - wave_float * wave_float, 1.0) / jnp.maximum(4.0 * lower_degree * lower_degree - 1.0, 1.0))
        upward = forward_coef * (cosine * previous - backward_coef * before_previous)
        column_value = jnp.where(degree == wave_grid, diagonal_start, jnp.where(degree == wave_grid + 1, jnp.sqrt(2.0 * wave_float + 3.0) * cosine * previous, jnp.where(degree > wave_grid + 1, upward, 0.0)))
        column_value = jnp.where(degree < wave_count, column_value, 0.0)
        return ((column_value, previous), column_value * weight)
    zero_state = jnp.zeros(diagonal_start.shape, jnp.float32)
    _, columns = lax.scan(advance, (zero_state, zero_state), jnp.arange(wave_count + 1, dtype=jnp.int32))
    return jnp.moveaxis(columns, 0, 3).astype(jnp.bfloat16)


def draw_basis(key, part):
    slots = wave_slots(key).reshape(-1, 2)
    block_pairs = math.gcd(PAIRS, 16)
    firsts = slots[:, 0].reshape(-1, block_pairs)
    seconds = slots[:, 1].reshape(-1, block_pairs)
    lat_index = jnp.arange(NLAT, dtype=jnp.int32)

    def one_block(item):
        return make_basis(item[0], item[1], lat_index, NLAT, WAVES)
    stacked = lax.map(one_block, (firsts, seconds))
    return stacked.reshape(PAIRS, 2, NLAT, WAVES + 1)


def draw_fields(key, part):
    keys = jax.random.split(jax.random.fold_in(key, 23), 9)
    mode_count = min(max(PAIRS // 8, 4), PAIRS)
    common_weight = 0.8
    wander_weight = 0.6
    memory = 0.9
    mode_wave = jax.random.permutation(keys[0], PAIRS)[:mode_count].astype(jnp.int32)
    amplitude = jnp.exp(jax.random.uniform(keys[1], (mode_count,), jnp.float32, math.log(0.3), math.log(1.5)))
    profile = jax.random.normal(keys[2], (mode_count, NLAT), jnp.float32)
    shift_angle = jax.random.uniform(keys[3], (mode_count, NLAT), jnp.float32, -math.pi, math.pi)
    lon_index = jnp.arange(NLON, dtype=jnp.int32)
    turns = (mode_wave[:, None] * lon_index[None, :] % NLON).astype(jnp.float32) * (2.0 * math.pi / NLON)
    pattern = amplitude[:, None, None] * profile[:, :, None] * jnp.cos(turns[:, None, :] + shift_angle[:, :, None])
    pattern_flat = pattern.reshape(mode_count, NLAT * NLON)
    loading = jax.random.normal(keys[4], (LEV, mode_count), jnp.float32)
    season_angle = jax.random.uniform(keys[5], (), jnp.float32, -math.pi, math.pi)
    time_float = jnp.arange(TIME, dtype=jnp.float32)
    seasonal = 1.0 + 0.5 * jnp.cos(2.0 * math.pi * time_float / TIME + season_angle)
    shocks = jax.random.normal(keys[6], (TIME, LEV, mode_count), jnp.float32)
    start_state = jax.random.normal(keys[7], (LEV, mode_count), jnp.float32)

    def evolve(state, shock):
        following = memory * state + math.sqrt(1.0 - memory * memory) * shock
        return (following, following)
    _, wander = lax.scan(evolve, start_state, shocks)
    series = common_weight * loading[None, :, :] * seasonal[:, None, None] + wander_weight * wander
    series = jnp.moveaxis(series, 0, 1).reshape(LEV * TIME, mode_count)
    row_scale = jnp.ones((LEV * TIME,), jnp.float32)
    row_keys = jax.random.split(keys[8], LEV * TIME)

    def one_row(item):
        row_series, row_key, scale_row = item
        signal = jnp.dot(row_series, pattern_flat).reshape(NLAT, NLON)
        noise = jax.random.normal(row_key, (NLAT, NLON), jnp.float32)
        return jnp.clip(0.3 * (signal + scale_row * noise), -4.0, 4.0).astype(jnp.bfloat16)
    rows = lax.map(one_row, (series, row_keys, row_scale))
    return rows.reshape(LEV, TIME, NLAT, NLON)


def setup_inputs(seed: int = 0) -> dict:
    splits = jax.random.split(jax.random.key(seed), 4)
    fields = draw_fields(jax.random.fold_in(splits[3], 71), 0)
    wave_order = draw_wave_order(jax.random.fold_in(splits[3], 71), 0)
    basis = draw_basis(jax.random.fold_in(splits[3], 71), 0)
    return dict(fields=fields, wave_order=wave_order, basis=basis)


def fourier_table(wave_order, lon_count):
    lon_index = jnp.arange(lon_count, dtype=jnp.int32)
    phase = lon_index[:, None] * wave_order[None, :].astype(jnp.int32) % lon_count
    angle_grid = phase.astype(jnp.float32) * (2.0 * math.pi / lon_count)
    stacked = jnp.stack([jnp.cos(angle_grid), -jnp.sin(angle_grid)], axis=2)
    return stacked.reshape(lon_count, -1).astype(jnp.bfloat16)

def reference(fields, wave_order, basis):
    level_count, time_count, lat_total, lon_count = fields.shape
    wave_count = lon_count // 2
    fourier = fourier_table(wave_order, lon_count)

    def transform(level_field):
        flat_rows = level_field.reshape(-1, lon_count)
        result = jnp.dot(flat_rows.astype(jnp.float32), fourier.astype(jnp.float32), preferred_element_type=jnp.float32).astype(jnp.bfloat16)
        return result.reshape(time_count, lat_total, wave_count // 2, 4)
    spectra = lax.map(transform, fields)
    spectra = jnp.moveaxis(spectra, 3, 0)

    def per_pair(pair_item):
        pair_block, legendre = pair_item
        pair_data = pair_block.reshape(level_count, time_count, lat_total, 2, 2).astype(jnp.float32)
        return jnp.einsum('ltahc,haj->lcjt', pair_data, legendre.astype(jnp.float32))
    coefficients = lax.map(per_pair, (spectra, basis))
    coefficients = jnp.moveaxis(coefficients, 0, 1)
    matrix = coefficients.reshape(-1, time_count)
    gram_matrix = lax.dot_general(matrix.astype(jnp.float32), matrix.astype(jnp.float32), (((0,), (0,)), ((), ())), precision=lax.Precision.HIGHEST, preferred_element_type=jnp.float32) / matrix.shape[0]
    lower_factor = jnp.linalg.cholesky(gram_matrix)
    inverse = jax.scipy.linalg.solve_triangular(lower_factor, jnp.eye(time_count, dtype=jnp.float32), lower=True)
    whitened = jnp.dot(matrix.astype(jnp.float32), inverse.T.astype(jnp.float32), precision=lax.Precision.HIGHEST, preferred_element_type=jnp.float32).astype(jnp.bfloat16)
    return (whitened.reshape(coefficients.shape), lower_factor.T)
```

```python
import math

import jax
import jax.numpy as jnp
from jax import lax
from jax.experimental import pallas as pl
from jax.experimental.pallas import tpu as pltpu
from jax.sharding import PartitionSpec as P

F32 = jnp.float32
BF16 = jnp.bfloat16
AXES = ("grp", "band")


def cos_sin_quarter(position, lon_count):
    quarter = lon_count / 4.0
    turn = jnp.floor((position + quarter / 2.0) * (1.0 / quarter))
    angle = (position - turn * quarter) * (2.0 * math.pi / lon_count)
    square = angle * angle
    cosine = 1.0 + square * (-0.5 + square * (1.0 / 24 + square * (-1.0 / 720 + square * (1.0 / 40320))))
    sine = angle * (1.0 + square * (-1.0 / 6 + square * (1.0 / 120 + square * (-1.0 / 5040 + square * (1.0 / 362880)))))
    odd = (turn == 1.0) | (turn == 3.0)
    first = jnp.where(odd, sine, cosine)
    second = jnp.where(odd, cosine, sine)
    first = jnp.where((turn == 1.0) | (turn == 2.0), -first, first)
    second = jnp.where((turn == 2.0) | (turn == 3.0), -second, second)
    return first, second


def wrap(value, period):
    return value - period * jnp.floor((value + 0.5) * (1.0 / period))


def build_table(wave_ref, table_ref, lon_count):
    rows = table_ref.shape[0]
    step_rows = 32
    lanes = 128
    half_blocks = lon_count // lanes // 2

    def body(index, carry):
        at = pl.ds(pl.multiple_of(index * step_rows, step_rows), step_rows)
        wave = wave_ref[at, :]
        lane = lax.broadcasted_iota(jnp.int32, wave.shape, 1).astype(F32)
        row = lax.broadcasted_iota(jnp.int32, wave.shape, 0)
        quarter = jnp.where(row % 2 == 1, lon_count / 4.0, 0.0)
        real, imag = cos_sin_quarter(wrap(wave * lane + quarter, float(lon_count)), lon_count)
        turn_real, turn_imag = cos_sin_quarter(wrap(wave * float(lanes), float(lon_count)), lon_count)
        sign = 1.0 - 2.0 * wrap(wave, 2.0)
        for block in range(half_blocks):
            table_ref[at, block * lanes:(block + 1) * lanes] = real.astype(BF16)
            other = block + half_blocks
            table_ref[at, other * lanes:(other + 1) * lanes] = (real * sign).astype(BF16)
            if block + 1 < half_blocks:
                real, imag = real * turn_real - imag * turn_imag, real * turn_imag + imag * turn_real
        return carry

    lax.fori_loop(0, rows // step_rows, body, 0)


def fourier_kernel(wave_ref, field_ref, out_ref, table_ref):
    lon_count = field_ref.shape[3]

    @pl.when((pl.program_id(0) == 0) & (pl.program_id(1) == 0))
    def _():
        build_table(wave_ref, table_ref, lon_count)

    field = field_ref[0, 0]
    pairs = out_ref.shape[3]
    rows = table_ref.shape[0] // pairs
    for pair in range(pairs):
        result = lax.dot_general(
            table_ref[pair * rows:(pair + 1) * rows, :], field, (((1,), (1,)), ((), ())), preferred_element_type=F32
        )
        left = result[:, :128].reshape(rows // 8, 8, 128)
        right = result[:, 128:].reshape(rows // 8, 8, 128)
        low = lax.broadcasted_iota(jnp.int32, left.shape, 1) < 4
        even = jnp.where(low, left, pltpu.roll(right, 4, 1))
        odd = jnp.where(low, pltpu.roll(left, 4, 1), right)
        mixed = jnp.stack([even, odd], axis=1).reshape(rows // 4, 8, 128)
        out_ref[0, :, 0, pair] = mixed.astype(BF16)


def transform(fields, waves, bands):
    levels, lats, times, lon_count = fields.shape
    pairs = waves.shape[0] // (bands * 4)
    return pl.pallas_call(
        fourier_kernel,
        grid=(levels, lats),
        in_specs=[
            pl.BlockSpec(waves.shape, lambda l, i: (0, 0)),
            pl.BlockSpec((1, 1, times, lon_count), lambda l, i: (l, i, 0, 0)),
        ],
        out_specs=pl.BlockSpec((1, bands, 1, pairs, 8, 128), lambda l, i: (l, 0, i, 0, 0, 0)),
        out_shape=jax.ShapeDtypeStruct((levels, bands, lats, pairs, 8, 128), BF16),
        scratch_shapes=[pltpu.VMEM((waves.shape[0], lon_count), BF16)],
        name="fourier",
    )(waves, fields)


def legendre_kernel(spectra_ref, basis_ref, high_ref, low_ref, gram_ref, wide_ref, side_ref, cross_ref):
    step = pl.program_id(0)

    @pl.when(step == 0)
    def _():
        gram_ref[...] = jnp.zeros_like(gram_ref)
        cross_ref[...] = jnp.zeros_like(cross_ref)

    lats = spectra_ref.shape[0]
    wide_ref[...] = spectra_ref[:, 0].astype(F32).reshape(lats * 8, 128)
    for half in range(2):
        for h in range(2):
            for c in range(2):
                piece = wide_ref[pl.ds(half * 4 + h * 2 + c, lats, stride=8), :]
                side_ref[h, :, c * 256 + half * 128:c * 256 + half * 128 + 128] = piece.astype(BF16)
    product = jnp.dot(basis_ref[0, 0], side_ref[0], preferred_element_type=F32)
    product += jnp.dot(basis_ref[0, 1], side_ref[1], preferred_element_type=F32)
    flip = (((0,), (0,)), ((), ()))
    for c in range(2):
        value = product[:, c * 256:(c + 1) * 256]
        high = value.astype(BF16)
        low = (value - high.astype(F32)).astype(BF16)
        high_ref[0, c] = high
        low_ref[0, c] = low
        gram_ref[...] += lax.dot_general(high, high, flip, preferred_element_type=F32)
        gram_ref[...] += lax.dot_general(low, low, flip, preferred_element_type=F32)
        cross_ref[...] += lax.dot_general(high, low, flip, preferred_element_type=F32)

    @pl.when(step == pl.num_programs(0) - 1)
    def _():
        gram_ref[...] += cross_ref[...] + cross_ref[...].T


def project(spectra, legendre):
    lats, pairs = spectra.shape[:2]
    rows = legendre.shape[2]
    coefficient = jax.ShapeDtypeStruct((pairs, 2, rows, 256), BF16)
    block = pl.BlockSpec((1, 2, rows, 256), lambda q: (q, 0, 0, 0))
    return pl.pallas_call(
        legendre_kernel,
        grid=(pairs,),
        in_specs=[
            pl.BlockSpec((lats, 1, 8, 128), lambda q: (0, q, 0, 0)),
            pl.BlockSpec((1, 2, rows, lats), lambda q: (q, 0, 0, 0)),
        ],
        out_specs=[block, block, pl.BlockSpec((256, 256), lambda q: (0, 0))],
        out_shape=[coefficient, coefficient, jax.ShapeDtypeStruct((256, 256), F32)],
        scratch_shapes=[
            pltpu.VMEM((lats * 8, 128), F32),
            pltpu.VMEM((2, lats, 512), BF16),
            pltpu.VMEM((256, 256), F32),
        ],
        name="legendre",
    )(spectra, legendre)


def whiten_kernel(high_ref, low_ref, inverse_ref, out_ref):
    rows = out_ref.shape[2]
    inverse = inverse_ref[...]
    inverse_high = inverse.astype(BF16)
    inverse_low = (inverse - inverse_high.astype(F32)).astype(BF16)
    across = (((1,), (1,)), ((), ()))
    for c in range(2):
        value = lax.dot_general(high_ref[0, c], inverse_high, across, preferred_element_type=F32)
        value += lax.dot_general(high_ref[0, c], inverse_low, across, preferred_element_type=F32)
        value += lax.dot_general(low_ref[0, c], inverse_high, across, preferred_element_type=F32)
        out_ref[0, c] = value[:rows].astype(BF16)


def whiten(high, low, inverse, degree_rows):
    pairs, _, rows, _ = high.shape
    block = pl.BlockSpec((1, 2, rows, 256), lambda q: (q, 0, 0, 0))
    return pl.pallas_call(
        whiten_kernel,
        grid=(pairs,),
        in_specs=[block, block, pl.BlockSpec((256, 256), lambda q: (0, 0))],
        out_specs=pl.BlockSpec((1, 2, degree_rows, 256), lambda q: (q, 0, 0, 0)),
        out_shape=jax.ShapeDtypeStruct((pairs, 2, degree_rows, 256), BF16),
        name="whiten",
    )(high, low, inverse)


def exchange(value):
    return lax.all_to_all(value, AXES, split_axis=0, concat_axis=0, tiled=True)


def reduce_gram(gram, devices):
    pieces = gram.reshape(devices, -1, 128)
    total = exchange(pieces).sum(axis=0, keepdims=True)
    return exchange(jnp.broadcast_to(total, pieces.shape)).reshape(gram.shape)


def shards(fields, wave_order, basis):
    levels, times, lats, lon_count = fields.shape
    groups, bands = lax.axis_size("grp"), lax.axis_size("band")
    pairs, _, lat_total, degree_rows = basis.shape
    padded_rows = -(-degree_rows // 16) * 16
    waves = wave_order.reshape(bands, pairs, 2).transpose(1, 0, 2).reshape(-1)
    waves = jnp.broadcast_to(jnp.repeat(waves, 2)[:, None], (waves.shape[0] * 2, 128)).astype(F32)
    sent = transform(fields.transpose(0, 2, 1, 3), waves, bands)
    received = exchange(sent.reshape(groups * bands, lats, pairs, 8, 128))
    legendre = jnp.pad(basis.transpose(0, 1, 3, 2), ((0, 0), (0, 0), (0, padded_rows - degree_rows), (0, 0)))
    high, low, local_gram = project(received.reshape(lat_total, pairs, 8, 128), legendre)
    total_rows = levels * pairs * bands * 2 * degree_rows
    gram_matrix = reduce_gram(local_gram, groups * bands) / total_rows
    lower_factor = jnp.linalg.cholesky(gram_matrix)
    inverse = jax.scipy.linalg.solve_triangular(lower_factor, jnp.eye(times, dtype=F32), lower=True)
    whitened = whiten(high, low, inverse, degree_rows)
    return (whitened[None], lower_factor.T)


def solution(mesh):
    placed = (P(None, None, ("grp", "band"), None), P(), P("band", None, None, None))
    return jax.shard_map(
        shards,
        mesh=mesh,
        in_specs=placed,
        out_specs=(P("grp", "band", None, None, None), P()),
        check_vma=False,
    )
```

```python
import functools
import math

import jax
import jax.numpy as jnp
from jax import lax
from jax.experimental import pallas as pl
from jax.experimental.pallas import tpu as pltpu
from jax.sharding import PartitionSpec as P

F32 = jnp.float32
BF16 = jnp.bfloat16
AXES = ("grp", "band")
CHUNKS = (2, 3)


def cos_sin_quarter(position, lon_count):
    quarter = lon_count / 4.0
    turn = jnp.floor((position + quarter / 2.0) * (1.0 / quarter))
    angle = (position - turn * quarter) * (2.0 * math.pi / lon_count)
    square = angle * angle
    cosine = 1.0 + square * (-0.5 + square * (1.0 / 24 + square * (-1.0 / 720 + square * (1.0 / 40320))))
    sine = angle * (1.0 + square * (-1.0 / 6 + square * (1.0 / 120 + square * (-1.0 / 5040 + square * (1.0 / 362880)))))
    odd = (turn == 1.0) | (turn == 3.0)
    first = jnp.where(odd, sine, cosine)
    second = jnp.where(odd, cosine, sine)
    first = jnp.where((turn == 1.0) | (turn == 2.0), -first, first)
    second = jnp.where((turn == 2.0) | (turn == 3.0), -second, second)
    return first, second


def wrap(value, period):
    return value - period * jnp.floor((value + 0.5) * (1.0 / period))


def build_table(chunk, pairs_total, orders_ref, wave_ref, table_ref, lon_count):
    start, pairs = chunk
    lanes = 128
    step_rows = 32
    half_blocks = lon_count // lanes // 2
    rows = table_ref.shape[0] // pairs
    orders = orders_ref[...].astype(F32)
    high = jnp.floor((orders + 0.5) * (1.0 / 32))
    low = orders - 32.0 * high
    high = jnp.broadcast_to(high, (lanes, high.shape[1])).astype(BF16)
    low = jnp.broadcast_to(low, (lanes, low.shape[1])).astype(BF16)
    shape = (rows, orders.shape[1])
    row = lax.broadcasted_iota(jnp.int32, shape, 0)
    slot = lax.broadcasted_iota(jnp.int32, shape, 1)
    across = (((1,), (1,)), ((), ()))
    for pair in range(pairs):
        wanted = (row // 4) * (2 * pairs_total) + 2 * (start + pair) + (row // 2) % 2
        choice = jnp.where(slot == wanted, 1.0, 0.0).astype(BF16)
        wave_ref[pair * rows:(pair + 1) * rows, :] = 32.0 * lax.dot_general(
            choice, high, across, preferred_element_type=F32
        ) + lax.dot_general(choice, low, across, preferred_element_type=F32)

    def body(index, carry):
        at = pl.ds(pl.multiple_of(index * step_rows, step_rows), step_rows)
        wave = wave_ref[at, :]
        lane = lax.broadcasted_iota(jnp.int32, wave.shape, 1).astype(F32)
        parity = lax.broadcasted_iota(jnp.int32, wave.shape, 0) % 2
        quarter = jnp.where(parity == 1, lon_count / 4.0, 0.0)
        real, imag = cos_sin_quarter(wrap(wave * lane + quarter, float(lon_count)), lon_count)
        turn_real, turn_imag = cos_sin_quarter(wrap(wave * float(lanes), float(lon_count)), lon_count)
        sign = 1.0 - 2.0 * wrap(wave, 2.0)
        for block in range(half_blocks):
            table_ref[at, block * lanes:(block + 1) * lanes] = real.astype(BF16)
            other = block + half_blocks
            table_ref[at, other * lanes:(other + 1) * lanes] = (real * sign).astype(BF16)
            if block + 1 < half_blocks:
                real, imag = real * turn_real - imag * turn_imag, real * turn_imag + imag * turn_real
        return carry

    lax.fori_loop(0, table_ref.shape[0] // step_rows, body, 0)


def fourier_kernel(chunk, pairs_total, orders_ref, field_ref, out_ref, wave_ref, table_ref):
    lon_count = field_ref.shape[3]

    @pl.when((pl.program_id(0) == 0) & (pl.program_id(1) == 0))
    def _():
        build_table(chunk, pairs_total, orders_ref, wave_ref, table_ref, lon_count)

    field = field_ref[0, 0]
    pairs = chunk[1]
    rows = table_ref.shape[0] // pairs
    for pair in range(pairs):
        result = lax.dot_general(
            table_ref[pair * rows:(pair + 1) * rows, :], field, (((1,), (1,)), ((), ())), preferred_element_type=F32
        )
        left = result[:, :128].reshape(rows // 8, 8, 128)
        right = result[:, 128:].reshape(rows // 8, 8, 128)
        low = lax.broadcasted_iota(jnp.int32, left.shape, 1) < 4
        even = jnp.where(low, left, pltpu.roll(right, 4, 1))
        odd = jnp.where(low, pltpu.roll(left, 4, 1), right)
        mixed = jnp.stack([even, odd], axis=1).reshape(rows // 4, 8, 128)
        out_ref[0, :, 0, pair] = mixed.astype(BF16)


def transform(fields, orders, bands, pairs_total, chunk):
    levels, lats, times, lon_count = fields.shape
    pairs = chunk[1]
    rows = pairs * bands * 4
    return pl.pallas_call(
        functools.partial(fourier_kernel, chunk, pairs_total),
        grid=(levels, lats),
        in_specs=[
            pl.BlockSpec(orders.shape, lambda l, i: (0, 0)),
            pl.BlockSpec((1, 1, times, lon_count), lambda l, i: (l, i, 0, 0)),
        ],
        out_specs=pl.BlockSpec((1, bands, 1, pairs, 8, 128), lambda l, i: (l, 0, i, 0, 0, 0)),
        out_shape=jax.ShapeDtypeStruct((levels, bands, lats, pairs, 8, 128), BF16),
        scratch_shapes=[pltpu.VMEM((rows, 128), F32), pltpu.VMEM((rows, lon_count), BF16)],
        cost_estimate=pl.CostEstimate(
            flops=2 * rows * levels * lats * times * lon_count,
            bytes_accessed=2 * levels * lats * times * (lon_count + rows),
            transcendentals=0,
        ),
        name="fourier",
    )(orders, fields)


def legendre_kernel(later, spectra_ref, basis_ref, *refs):
    if later:
        before_ref, refs = refs[2], refs[3:]
    high_ref, low_ref, gram_ref, wide_ref, side_ref, cross_ref = refs
    step = pl.program_id(0)

    @pl.when(step == 0)
    def _():
        gram_ref[...] = before_ref[...] if later else jnp.zeros_like(gram_ref)
        cross_ref[...] = jnp.zeros_like(cross_ref)

    lats = spectra_ref.shape[0]
    wide_ref[...] = spectra_ref[:, 0].astype(F32).reshape(lats * 8, 128)
    for half in range(2):
        for h in range(2):
            for c in range(2):
                piece = wide_ref[pl.ds(half * 4 + h * 2 + c, lats, stride=8), :]
                side_ref[h, :, c * 256 + half * 128:c * 256 + half * 128 + 128] = piece.astype(BF16)
    product = jnp.dot(basis_ref[0, 0], side_ref[0], preferred_element_type=F32)
    product += jnp.dot(basis_ref[0, 1], side_ref[1], preferred_element_type=F32)
    flip = (((0,), (0,)), ((), ()))
    for c in range(2):
        value = product[:, c * 256:(c + 1) * 256]
        high = value.astype(BF16)
        low = (value - high.astype(F32)).astype(BF16)
        high_ref[0, c] = high
        low_ref[0, c] = low
        gram_ref[...] += lax.dot_general(high, high, flip, preferred_element_type=F32)
        gram_ref[...] += lax.dot_general(low, low, flip, preferred_element_type=F32)
        cross_ref[...] += lax.dot_general(high, low, flip, preferred_element_type=F32)

    @pl.when(step == pl.num_programs(0) - 1)
    def _():
        gram_ref[...] += cross_ref[...] + cross_ref[...].T


def project(spectra, legendre, start, carried):
    lats, pairs = spectra.shape[:2]
    pairs_total, _, rows, _ = legendre.shape
    coefficient = jax.ShapeDtypeStruct((pairs_total, 2, rows, 256), BF16)
    block = pl.BlockSpec((1, 2, rows, 256), lambda q: (q + start, 0, 0, 0))
    whole = pl.BlockSpec((256, 256), lambda q: (0, 0))
    later = carried is not None
    kept = pl.BlockSpec(memory_space=pl.ANY)
    return pl.pallas_call(
        functools.partial(legendre_kernel, later),
        grid=(pairs,),
        in_specs=[
            pl.BlockSpec((lats, 1, 8, 128), lambda q: (0, q, 0, 0)),
            pl.BlockSpec((1, 2, rows, lats), lambda q: (q + start, 0, 0, 0)),
        ] + ([kept, kept, whole] if later else []),
        out_specs=[block, block, whole],
        out_shape=[coefficient, coefficient, jax.ShapeDtypeStruct((256, 256), F32)],
        scratch_shapes=[
            pltpu.VMEM((lats * 8, 128), F32),
            pltpu.VMEM((2, lats, 512), BF16),
            pltpu.VMEM((256, 256), F32),
        ],
        input_output_aliases={2: 0, 3: 1} if later else {},
        cost_estimate=pl.CostEstimate(
            flops=pairs * (4 * rows * lats * 512 + 12 * rows * 256 * 256),
            bytes_accessed=pairs * (lats * 2048 + 4 * rows * lats + rows * 2048),
            transcendentals=0,
        ),
        name="legendre",
    )(spectra, legendre, *(carried or ()))


def factor_block(groups):
    count = len(groups)
    n = count * 8
    shape = (8, n)
    lane = lax.broadcasted_iota(jnp.int32, shape, 1)
    sub = lax.broadcasted_iota(jnp.int32, shape, 0)
    work = list(groups)
    upper, inverse = [jnp.zeros(shape, F32)] * count, [jnp.zeros(shape, F32)] * count
    for j in range(0, n, 2):
        g, r = divmod(j, 8)
        col0 = [jnp.broadcast_to(work[k][:, j:j + 1], shape) for k in range(g, count)]
        col1 = [jnp.broadcast_to(work[k][:, j + 1:j + 2], shape) for k in range(g, count)]
        p = jnp.broadcast_to(col0[0][r:r + 1], shape)
        q = jnp.broadcast_to(col0[0][r + 1:r + 2], shape)
        s = jnp.broadcast_to(col1[0][r + 1:r + 2], shape)
        row0 = jnp.broadcast_to(work[g][r:r + 1], shape)
        row1 = jnp.broadcast_to(work[g][r + 1:r + 2], shape)
        over0 = 1.0 / p
        ratio = q * over0
        rest = s - q * ratio
        over1 = 1.0 / rest
        first, second = lane == j, lane == j + 1
        unit0 = jnp.where(first, 1.0, jnp.where(second, 0.0, row0))
        unit1 = jnp.where(second, 1.0, jnp.where(first, 0.0, row1)) - ratio * unit0
        down0, down1 = unit0 * over0, unit1 * over1
        pair = first | second
        for k in range(g, count):
            moved = jnp.where(pair, 0.0, work[k]) - col0[k - g] * down0 - (col1[k - g] - ratio * col0[k - g]) * down1
            work[k] = moved if k > g else jnp.where(sub > r + 1, moved, work[k])
        root0, root1 = lax.rsqrt(p), lax.rsqrt(rest)
        up0 = jnp.where(lane >= j, row0, 0.0) * root0
        up1 = jnp.where(lane >= j + 1, row1 - ratio * row0, 0.0) * root1
        inv0 = jnp.where(lane <= j, unit0, 0.0) * root0
        inv1 = jnp.where(lane <= j + 1, unit1, 0.0) * root1
        upper[g] = jnp.where(sub == r, up0, jnp.where(sub == r + 1, up1, upper[g]))
        inverse[g] = jnp.where(sub == r, inv0, jnp.where(sub == r + 1, inv1, inverse[g]))
    return jnp.concatenate(upper, 0), jnp.concatenate(inverse, 0)


def f32_dot(a, b, dims=(((1,), (0,)), ((), ()))):
    return lax.dot_general(a, b, dims, precision=lax.Precision.HIGHEST, preferred_element_type=F32)


def factor_into(scale, gram_ref, factor_ref, inverse_ref, block_ref):
    half = gram_ref.shape[0] // 2
    flip = (((0,), (0,)), ((), ()))
    block_ref[...] = gram_ref[:half, :half] * scale

    def step(index, carry):
        upper, inverse = factor_block([block_ref[k * 8:(k + 1) * 8, :] for k in range(half // 8)])

        @pl.when(index == 0)
        def _():
            factor_ref[:half, :half] = upper
            inverse_ref[:half, :half] = inverse
            side = f32_dot(inverse, gram_ref[:half, half:] * scale)
            factor_ref[:half, half:] = side
            block_ref[...] = gram_ref[half:, half:] * scale - f32_dot(side, side, flip)

        @pl.when(index == 1)
        def _():
            factor_ref[half:, half:] = upper
            inverse_ref[half:, half:] = inverse
            below = f32_dot(factor_ref[:half, half:], inverse_ref[:half, :half], flip)
            inverse_ref[half:, :half] = -f32_dot(inverse, below)

        return carry

    lax.fori_loop(0, 2, step, 0)
    factor_ref[half:, :half] = jnp.zeros((half, half), F32)
    inverse_ref[:half, half:] = jnp.zeros((half, half), F32)


def finish_kernel(scale, gram_ref, high_ref, low_ref, out_ref, factor_ref, inverse_ref, block_ref, top_ref, rest_ref):
    @pl.when(pl.program_id(0) == 0)
    def _():
        factor_into(scale, gram_ref, factor_ref, inverse_ref, block_ref)
        inverse = inverse_ref[...]
        top = inverse.astype(BF16)
        top_ref[...] = top
        rest_ref[...] = (inverse - top.astype(F32)).astype(BF16)

    rows = out_ref.shape[1]
    across = (((1,), (1,)), ((), ()))
    for c in range(2):
        value = lax.dot_general(high_ref[0, c], top_ref[...], across, preferred_element_type=F32)
        value += lax.dot_general(high_ref[0, c], rest_ref[...], across, preferred_element_type=F32)
        value += lax.dot_general(low_ref[0, c], top_ref[...], across, preferred_element_type=F32)
        out_ref[0, :, c, :] = value[:rows].astype(BF16)


def finish(gram, high, low, total_rows, degree_rows):
    pairs, _, rows, _ = high.shape
    block = pl.BlockSpec((1, 2, rows, 256), lambda q: (q, 0, 0, 0))
    whole = pl.BlockSpec((256, 256), lambda q: (0, 0))
    return pl.pallas_call(
        functools.partial(finish_kernel, 1.0 / total_rows),
        grid=(pairs,),
        in_specs=[whole, block, block],
        out_specs=[pl.BlockSpec((1, degree_rows, 2, 256), lambda q: (q, 0, 0, 0)), whole],
        out_shape=[
            jax.ShapeDtypeStruct((pairs, degree_rows, 2, 256), BF16),
            jax.ShapeDtypeStruct((256, 256), F32),
        ],
        scratch_shapes=[
            pltpu.VMEM((256, 256), F32),
            pltpu.VMEM((128, 128), F32),
            pltpu.VMEM((256, 256), BF16),
            pltpu.VMEM((256, 256), BF16),
        ],
        name="finish",
    )(gram, high, low)


def exchange(value):
    return lax.all_to_all(value, AXES, split_axis=0, concat_axis=0, tiled=True)


def reduce_gram(gram, devices):
    pieces = gram.reshape(devices, -1, 128)
    total = exchange(pieces).sum(axis=0, keepdims=True)
    return exchange(jnp.broadcast_to(total, pieces.shape)).reshape(gram.shape)


def shards(fields, wave_order, basis):
    levels, times, lats, lon_count = fields.shape
    groups, bands = lax.axis_size("grp"), lax.axis_size("band")
    pairs, _, lat_total, degree_rows = basis.shape
    padded_rows = -(-degree_rows // 16) * 16
    fields = fields.transpose(0, 2, 1, 3)
    orders = wave_order.reshape(1, -1)
    starts = [sum(CHUNKS[:n]) for n in range(len(CHUNKS))]
    received = []
    for chunk in zip(starts, CHUNKS):
        sent = transform(fields, orders, bands, pairs, chunk)
        received.append(exchange(sent.reshape(groups * bands, lats, chunk[1], 8, 128)))
    legendre = jnp.pad(basis.transpose(0, 1, 3, 2), ((0, 0), (0, 0), (0, padded_rows - degree_rows), (0, 0)))
    carried = None
    for start, spectra in zip(starts, received):
        carried = project(spectra.reshape(lat_total, -1, 8, 128), legendre, start, carried)
    high, low, local_gram = carried
    gram = reduce_gram(local_gram, groups * bands)
    whitened, factor = finish(gram, high, low, levels * pairs * bands * 2 * degree_rows, degree_rows)
    return (whitened.transpose(0, 2, 1, 3)[None], factor)


def solution(mesh):
    placed = (P(None, None, ("grp", "band"), None), P(), P("band", None, None, None))
    return jax.shard_map(
        shards,
        mesh=mesh,
        in_specs=placed,
        out_specs=(P("grp", "band", None, None, None), P()),
        check_vma=False,
    )
```

```python
import functools
import math

import jax
import jax.numpy as jnp
from jax import lax
from jax.experimental import pallas as pl
from jax.experimental.pallas import tpu as pltpu
from jax.sharding import PartitionSpec as P

F32 = jnp.float32
BF16 = jnp.bfloat16
AXES = ("grp", "band")
CHUNKS = (1, 4)


def cos_sin_quarter(position, lon_count):
    quarter = lon_count / 4.0
    turn = jnp.floor((position + quarter / 2.0) * (1.0 / quarter))
    angle = (position - turn * quarter) * (2.0 * math.pi / lon_count)
    square = angle * angle
    cosine = 1.0 + square * (-0.5 + square * (1.0 / 24 + square * (-1.0 / 720 + square * (1.0 / 40320))))
    sine = angle * (1.0 + square * (-1.0 / 6 + square * (1.0 / 120 + square * (-1.0 / 5040 + square * (1.0 / 362880)))))
    odd = (turn == 1.0) | (turn == 3.0)
    first = jnp.where(odd, sine, cosine)
    second = jnp.where(odd, cosine, sine)
    first = jnp.where((turn == 1.0) | (turn == 2.0), -first, first)
    second = jnp.where((turn == 2.0) | (turn == 3.0), -second, second)
    return first, second


def wrap(value, period):
    return value - period * jnp.floor((value + 0.5) * (1.0 / period))


def build_table(chunk, pairs_total, orders_ref, wave_ref, table_ref, lon_count):
    start, pairs = chunk
    lanes = 128
    step_rows = 32
    half_blocks = lon_count // lanes // 2
    rows = table_ref.shape[0] // pairs
    orders = orders_ref[...].astype(F32).reshape(1, -1)
    high = jnp.floor((orders + 0.5) * (1.0 / 32))
    low = orders - 32.0 * high
    high = jnp.broadcast_to(high, (lanes, high.shape[1])).astype(BF16)
    low = jnp.broadcast_to(low, (lanes, low.shape[1])).astype(BF16)
    shape = (rows, orders.shape[1])
    row = lax.broadcasted_iota(jnp.int32, shape, 0)
    slot = lax.broadcasted_iota(jnp.int32, shape, 1)
    across = (((1,), (1,)), ((), ()))
    for pair in range(pairs):
        wanted = (row // 4) * (2 * pairs_total) + 2 * (start + pair) + (row // 2) % 2
        choice = jnp.where(slot == wanted, 1.0, 0.0).astype(BF16)
        wave_ref[pair * rows:(pair + 1) * rows, :] = 32.0 * lax.dot_general(
            choice, high, across, preferred_element_type=F32
        ) + lax.dot_general(choice, low, across, preferred_element_type=F32)

    def body(index, carry):
        at = pl.ds(pl.multiple_of(index * step_rows, step_rows), step_rows)
        wave = wave_ref[at, :]
        lane = lax.broadcasted_iota(jnp.int32, wave.shape, 1).astype(F32)
        parity = lax.broadcasted_iota(jnp.int32, wave.shape, 0) % 2
        quarter = jnp.where(parity == 1, lon_count / 4.0, 0.0)
        real, imag = cos_sin_quarter(wrap(wave * lane + quarter, float(lon_count)), lon_count)
        turn_real, turn_imag = cos_sin_quarter(wrap(wave * float(lanes), float(lon_count)), lon_count)
        sign = 1.0 - 2.0 * wrap(wave, 2.0)
        for block in range(half_blocks):
            table_ref[at, block * lanes:(block + 1) * lanes] = real.astype(BF16)
            other = block + half_blocks
            table_ref[at, other * lanes:(other + 1) * lanes] = (real * sign).astype(BF16)
            if block + 1 < half_blocks:
                real, imag = real * turn_real - imag * turn_imag, real * turn_imag + imag * turn_real
        return carry

    lax.fori_loop(0, table_ref.shape[0] // step_rows, body, 0)


def fourier_kernel(chunk, pairs_total, orders_ref, field_ref, out_ref, wave_ref, table_ref):
    lon_count = field_ref.shape[3]

    @pl.when(pl.program_id(0) == 0)
    def _():
        build_table(chunk, pairs_total, orders_ref, wave_ref, table_ref, lon_count)

    pairs = chunk[1]
    rows = table_ref.shape[0] // pairs
    for level in range(field_ref.shape[0]):
        field = field_ref[level, 0]
        whole = lax.dot_general(table_ref[...], field, (((1,), (1,)), ((), ())), preferred_element_type=F32)
        for pair in range(pairs):
            result = whole[pair * rows:(pair + 1) * rows]
            left = result[:, :128].reshape(rows // 8, 8, 128)
            right = result[:, 128:].reshape(rows // 8, 8, 128)
            low = lax.broadcasted_iota(jnp.int32, left.shape, 1) < 4
            even = jnp.where(low, left, pltpu.roll(right, 4, 1))
            odd = jnp.where(low, pltpu.roll(left, 4, 1), right)
            mixed = jnp.stack([even, odd], axis=1).reshape(rows // 4, 8, 128)
            out_ref[level, :, 0, pair] = mixed.astype(BF16)


def transform(fields, orders, bands, pairs_total, chunk):
    levels, lats, times, lon_count = fields.shape
    pairs = chunk[1]
    rows = pairs * bands * 4
    return pl.pallas_call(
        functools.partial(fourier_kernel, chunk, pairs_total),
        grid=(lats,),
        in_specs=[
            pl.BlockSpec(orders.shape, lambda i: (0,)),
            pl.BlockSpec((levels, 1, times, lon_count), lambda i: (0, i, 0, 0)),
        ],
        out_specs=pl.BlockSpec((levels, bands, 1, pairs, 8, 128), lambda i: (0, 0, i, 0, 0, 0)),
        out_shape=jax.ShapeDtypeStruct((levels, bands, lats, pairs, 8, 128), BF16),
        scratch_shapes=[pltpu.VMEM((rows, 128), F32), pltpu.VMEM((rows, lon_count), BF16)],
        cost_estimate=pl.CostEstimate(
            flops=2 * rows * levels * lats * times * lon_count,
            bytes_accessed=2 * levels * lats * times * (lon_count + rows),
            transcendentals=0,
        ),
        name="fourier",
    )(orders, fields)


def legendre_kernel(later, spectra_ref, basis_ref, *refs):
    if later:
        before_ref, refs = refs[2], refs[3:]
    high_ref, low_ref, gram_ref, wide_ref, side_ref, cross_ref = refs
    step = pl.program_id(0)

    @pl.when(step == 0)
    def _():
        gram_ref[...] = before_ref[...] if later else jnp.zeros_like(gram_ref)
        cross_ref[...] = jnp.zeros_like(cross_ref)

    lats = spectra_ref.shape[0]
    wide_ref[...] = spectra_ref[:, 0].astype(F32).reshape(lats * 8, 128)
    for half in range(2):
        for h in range(2):
            for c in range(2):
                piece = wide_ref[pl.ds(half * 4 + h * 2 + c, lats, stride=8), :]
                side_ref[h, :, c * 256 + half * 128:c * 256 + half * 128 + 128] = piece.astype(BF16)
    product = jnp.dot(basis_ref[0, 0], side_ref[0], preferred_element_type=F32)
    product += jnp.dot(basis_ref[0, 1], side_ref[1], preferred_element_type=F32)
    flip = (((0,), (0,)), ((), ()))
    for c in range(2):
        value = product[:, c * 256:(c + 1) * 256]
        high = value.astype(BF16)
        low = (value - high.astype(F32)).astype(BF16)
        high_ref[0, c] = high
        low_ref[0, c] = low
        gram_ref[...] += lax.dot_general(high, high, flip, preferred_element_type=F32)
        gram_ref[...] += lax.dot_general(low, low, flip, preferred_element_type=F32)
        cross_ref[...] += lax.dot_general(high, low, flip, preferred_element_type=F32)

    @pl.when(step == pl.num_programs(0) - 1)
    def _():
        gram_ref[...] += cross_ref[...] + cross_ref[...].T


def project(spectra, legendre, start, carried):
    lats, pairs = spectra.shape[:2]
    pairs_total, _, rows, _ = legendre.shape
    coefficient = jax.ShapeDtypeStruct((pairs_total, 2, rows, 256), BF16)
    block = pl.BlockSpec((1, 2, rows, 256), lambda q: (q + start, 0, 0, 0))
    whole = pl.BlockSpec((256, 256), lambda q: (0, 0))
    later = carried is not None
    kept = pl.BlockSpec(memory_space=pl.ANY)
    return pl.pallas_call(
        functools.partial(legendre_kernel, later),
        grid=(pairs,),
        in_specs=[
            pl.BlockSpec((lats, 1, 8, 128), lambda q: (0, q, 0, 0)),
            pl.BlockSpec((1, 2, rows, lats), lambda q: (q + start, 0, 0, 0)),
        ] + ([kept, kept, whole] if later else []),
        out_specs=[block, block, whole],
        out_shape=[coefficient, coefficient, jax.ShapeDtypeStruct((256, 256), F32)],
        scratch_shapes=[
            pltpu.VMEM((lats * 8, 128), F32),
            pltpu.VMEM((2, lats, 512), BF16),
            pltpu.VMEM((256, 256), F32),
        ],
        input_output_aliases={2: 0, 3: 1} if later else {},
        cost_estimate=pl.CostEstimate(
            flops=pairs * (4 * rows * lats * 512 + 12 * rows * 256 * 256),
            bytes_accessed=pairs * (lats * 2048 + 4 * rows * lats + rows * 2048),
            transcendentals=0,
        ),
        name="legendre",
    )(spectra, legendre, *(carried or ()))


def factor_block(groups, width):
    count = len(groups)
    n = count * 8
    shape = (8, n)
    lane = lax.broadcasted_iota(jnp.int32, shape, 1)
    sub = lax.broadcasted_iota(jnp.int32, shape, 0)
    work = list(groups)
    upper, inverse = [jnp.zeros(shape, F32)] * count, [jnp.zeros(shape, F32)] * count
    for j in range(0, n, width):
        g, r = divmod(j, 8)
        inside = (lane >= j) & (lane < j + width)
        cols = [
            [jnp.broadcast_to(work[k][:, j + a:j + a + 1], shape) for a in range(width)] for k in range(g, count)
        ]
        unit, plain, pivot, over, ratio = [], [], [], [], {}
        entry = {
            (b, a): jnp.broadcast_to(cols[0][a][r + b:r + b + 1], shape) for a in range(width) for b in range(a, width)
        }
        for a in range(width):
            pivot.append(entry[a, a])
            over.append(1.0 / pivot[a])
            for b in range(a + 1, width):
                ratio[b, a] = entry[b, a] * over[a]
            for b in range(a + 1, width):
                for e in range(b, width):
                    entry[e, b] = entry[e, b] - ratio[e, a] * entry[b, a]
        for a in range(width):
            row = jnp.broadcast_to(work[g][r + a:r + a + 1], shape)
            start = jnp.where(inside, jnp.where(lane == j + a, 1.0, 0.0), row)
            for b in range(a):
                row = row - ratio[a, b] * plain[b]
                start = start - ratio[a, b] * unit[b]
            plain.append(row)
            unit.append(start)
        down = [unit[a] * over[a] for a in range(width)]
        for k in range(g, count):
            if k == g and r + width == 8:
                continue
            moved = jnp.where(inside, 0.0, work[k])
            reduced = []
            for a in range(width):
                value = cols[k - g][a]
                for b in range(a):
                    value = value - ratio[a, b] * reduced[b]
                reduced.append(value)
                moved = moved - value * down[a]
            work[k] = moved if k > g else jnp.where(sub >= r + width, moved, work[k])
        for a in range(width):
            root = lax.rsqrt(pivot[a])
            up = jnp.where(lane >= j + a, plain[a], 0.0) * root
            inv = jnp.where(lane <= j + a, unit[a], 0.0) * root
            upper[g] = jnp.where(sub == r + a, up, upper[g])
            inverse[g] = jnp.where(sub == r + a, inv, inverse[g])
    return jnp.concatenate(upper, 0), jnp.concatenate(inverse, 0)


def f32_dot(a, b, dims=(((1,), (0,)), ((), ()))):
    return lax.dot_general(a, b, dims, precision=lax.Precision.HIGHEST, preferred_element_type=F32)


def factor_into(scale, gram_ref, factor_ref, inverse_ref, block_ref):
    half = gram_ref.shape[0] // 2
    flip = (((0,), (0,)), ((), ()))
    block_ref[...] = gram_ref[:half, :half] * scale

    def step(index, carry):
        upper, inverse = factor_block([block_ref[k * 8:(k + 1) * 8, :] for k in range(half // 8)], 8)

        @pl.when(index == 0)
        def _():
            factor_ref[:half, :half] = upper
            inverse_ref[:half, :half] = inverse
            side = f32_dot(inverse, gram_ref[:half, half:] * scale)
            factor_ref[:half, half:] = side
            block_ref[...] = gram_ref[half:, half:] * scale - f32_dot(side, side, flip)

        @pl.when(index == 1)
        def _():
            factor_ref[half:, half:] = upper
            inverse_ref[half:, half:] = inverse
            below = f32_dot(factor_ref[:half, half:], inverse_ref[:half, :half], flip)
            inverse_ref[half:, :half] = -f32_dot(inverse, below)

        return carry

    lax.fori_loop(0, 2, step, 0)
    factor_ref[half:, :half] = jnp.zeros((half, half), F32)
    inverse_ref[:half, half:] = jnp.zeros((half, half), F32)


def finish_kernel(
    scale, gram_ref, high_any, low_any, out_ref, factor_ref, inverse_ref, block_ref, top_ref, rest_ref, part_ref, sems
):
    pair = pl.program_id(0)
    pairs = part_ref.shape[1]

    def fetch(side, index):
        source = low_any if side else high_any
        return pltpu.make_async_copy(source.at[index], part_ref.at[side, index], sems.at[side, index])

    @pl.when(pair == 0)
    def _():
        for index in range(pairs):
            fetch(0, index).start()
            fetch(1, index).start()
        factor_into(scale, gram_ref, factor_ref, inverse_ref, block_ref)
        inverse = inverse_ref[...]
        top = inverse.astype(BF16)
        top_ref[...] = top
        rest_ref[...] = (inverse - top.astype(F32)).astype(BF16)

    fetch(0, pair).wait()
    fetch(1, pair).wait()
    across = (((1,), (1,)), ((), ()))
    for c in range(2):
        high, low = part_ref[0, pair, c], part_ref[1, pair, c]
        value = lax.dot_general(high, top_ref[...], across, preferred_element_type=F32)
        value += lax.dot_general(high, rest_ref[...], across, preferred_element_type=F32)
        value += lax.dot_general(low, top_ref[...], across, preferred_element_type=F32)
        out_ref[0, :, c, :] = value.astype(BF16)


def finish(gram, high, low, total_rows):
    pairs, _, degree_rows, _ = high.shape
    kept = pl.BlockSpec(memory_space=pl.ANY)
    whole = pl.BlockSpec((256, 256), lambda q: (0, 0))
    return pl.pallas_call(
        functools.partial(finish_kernel, 1.0 / total_rows),
        grid=(pairs,),
        in_specs=[whole, kept, kept],
        out_specs=[pl.BlockSpec((1, degree_rows, 2, 256), lambda q: (q, 0, 0, 0)), whole],
        out_shape=[
            jax.ShapeDtypeStruct((pairs, degree_rows, 2, 256), BF16),
            jax.ShapeDtypeStruct((256, 256), F32),
        ],
        scratch_shapes=[
            pltpu.VMEM((256, 256), F32),
            pltpu.VMEM((128, 128), F32),
            pltpu.VMEM((256, 256), BF16),
            pltpu.VMEM((256, 256), BF16),
            pltpu.VMEM((2, pairs, 2, degree_rows, 256), BF16),
            pltpu.SemaphoreType.DMA((2, pairs)),
        ],
        name="finish",
    )(gram, high, low)


def exchange(value):
    return lax.all_to_all(value, AXES, split_axis=0, concat_axis=0, tiled=True)


def reduce_gram(gram, devices):
    pieces = gram.reshape(devices, -1, 128)
    total = exchange(pieces).sum(axis=0, keepdims=True)
    return exchange(jnp.broadcast_to(total, pieces.shape)).reshape(gram.shape)


def shards(fields, wave_order, basis):
    levels, times, lats, lon_count = fields.shape
    groups, bands = lax.axis_size("grp"), lax.axis_size("band")
    pairs, _, lat_total, degree_rows = basis.shape
    fields = fields.transpose(0, 2, 1, 3)
    orders = wave_order
    starts = [sum(CHUNKS[:n]) for n in range(len(CHUNKS))]
    received = []
    for chunk in zip(starts, CHUNKS):
        sent = transform(fields, orders, bands, pairs, chunk)
        received.append(exchange(sent.reshape(groups * bands, lats, chunk[1], 8, 128)))
    legendre = basis.transpose(0, 1, 3, 2)
    carried = None
    for start, spectra in zip(starts, received):
        carried = project(spectra.reshape(lat_total, -1, 8, 128), legendre, start, carried)
    high, low, local_gram = carried
    gram = reduce_gram(local_gram, groups * bands)
    whitened, factor = finish(gram, high, low, levels * pairs * bands * 2 * degree_rows)
    return (whitened.transpose(0, 2, 1, 3)[None], factor)


def solution(mesh):
    placed = (P(None, None, ("grp", "band"), None), P(), P("band", None, None, None))
    return jax.shard_map(
        shards,
        mesh=mesh,
        in_specs=placed,
        out_specs=(P("grp", "band", None, None, None), P()),
        check_vma=False,
    )
```

```python
import functools
import math

import jax
import jax.numpy as jnp
from jax import lax
from jax.experimental import pallas as pl
from jax.experimental.pallas import tpu as pltpu
from jax.sharding import PartitionSpec as P

F32 = jnp.float32
BF16 = jnp.bfloat16
AXES = ("grp", "band")
CHUNKS = (1, 4)


def cos_sin_quarter(position, lon_count):
    quarter = lon_count / 4.0
    turn = jnp.floor((position + quarter / 2.0) * (1.0 / quarter))
    angle = (position - turn * quarter) * (2.0 * math.pi / lon_count)
    square = angle * angle
    cosine = 1.0 + square * (-0.5 + square * (1.0 / 24 + square * (-1.0 / 720 + square * (1.0 / 40320))))
    sine = angle * (1.0 + square * (-1.0 / 6 + square * (1.0 / 120 + square * (-1.0 / 5040 + square * (1.0 / 362880)))))
    odd = (turn == 1.0) | (turn == 3.0)
    first = jnp.where(odd, sine, cosine)
    second = jnp.where(odd, cosine, sine)
    first = jnp.where((turn == 1.0) | (turn == 2.0), -first, first)
    second = jnp.where((turn == 2.0) | (turn == 3.0), -second, second)
    return first, second


def wrap(value, period):
    return value - period * jnp.floor((value + 0.5) * (1.0 / period))


def build_table(chunk, pairs_total, orders_ref, wave_ref, table_ref, lon_count):
    start, pairs = chunk
    lanes = 128
    step_rows = 32
    half_blocks = lon_count // lanes // 2
    rows = table_ref.shape[0] // pairs
    orders = orders_ref[...].astype(F32).reshape(1, -1)
    high = jnp.floor((orders + 0.5) * (1.0 / 32))
    low = orders - 32.0 * high
    high = jnp.broadcast_to(high, (lanes, high.shape[1])).astype(BF16)
    low = jnp.broadcast_to(low, (lanes, low.shape[1])).astype(BF16)
    shape = (rows, orders.shape[1])
    row = lax.broadcasted_iota(jnp.int32, shape, 0)
    slot = lax.broadcasted_iota(jnp.int32, shape, 1)
    across = (((1,), (1,)), ((), ()))
    for pair in range(pairs):
        wanted = (row // 4) * (2 * pairs_total) + 2 * (start + pair) + (row // 2) % 2
        choice = jnp.where(slot == wanted, 1.0, 0.0).astype(BF16)
        wave_ref[pair * rows:(pair + 1) * rows, :] = 32.0 * lax.dot_general(
            choice, high, across, preferred_element_type=F32
        ) + lax.dot_general(choice, low, across, preferred_element_type=F32)

    def body(index, carry):
        at = pl.ds(pl.multiple_of(index * step_rows, step_rows), step_rows)
        wave = wave_ref[at, :]
        lane = lax.broadcasted_iota(jnp.int32, wave.shape, 1).astype(F32)
        parity = lax.broadcasted_iota(jnp.int32, wave.shape, 0) % 2
        quarter = jnp.where(parity == 1, lon_count / 4.0, 0.0)
        real, imag = cos_sin_quarter(wrap(wave * lane + quarter, float(lon_count)), lon_count)
        turn_real, turn_imag = cos_sin_quarter(wrap(wave * float(lanes), float(lon_count)), lon_count)
        sign = 1.0 - 2.0 * wrap(wave, 2.0)
        for block in range(half_blocks):
            table_ref[at, block * lanes:(block + 1) * lanes] = real.astype(BF16)
            other = block + half_blocks
            table_ref[at, other * lanes:(other + 1) * lanes] = (real * sign).astype(BF16)
            if block + 1 < half_blocks:
                real, imag = real * turn_real - imag * turn_imag, real * turn_imag + imag * turn_real
        return carry

    lax.fori_loop(0, table_ref.shape[0] // step_rows, body, 0)


def fourier_kernel(chunk, pairs_total, orders_ref, field_ref, out_ref, wave_ref, table_ref):
    lon_count = field_ref.shape[3]

    @pl.when(pl.program_id(0) == 0)
    def _():
        build_table(chunk, pairs_total, orders_ref, wave_ref, table_ref, lon_count)

    pairs = chunk[1]
    rows = table_ref.shape[0] // pairs
    for level in range(field_ref.shape[0]):
        field = field_ref[level, 0]
        whole = lax.dot_general(table_ref[...], field, (((1,), (1,)), ((), ())), preferred_element_type=F32)
        for pair in range(pairs):
            result = whole[pair * rows:(pair + 1) * rows]
            left = result[:, :128].reshape(rows // 8, 8, 128)
            right = result[:, 128:].reshape(rows // 8, 8, 128)
            low = lax.broadcasted_iota(jnp.int32, left.shape, 1) < 4
            even = jnp.where(low, left, pltpu.roll(right, 4, 1))
            odd = jnp.where(low, pltpu.roll(left, 4, 1), right)
            mixed = jnp.stack([even, odd], axis=1).reshape(rows // 4, 8, 128)
            out_ref[level, :, 0, pair] = mixed.astype(BF16)


def transform(fields, orders, bands, pairs_total, chunk):
    levels, lats, times, lon_count = fields.shape
    pairs = chunk[1]
    rows = pairs * bands * 4
    return pl.pallas_call(
        functools.partial(fourier_kernel, chunk, pairs_total),
        grid=(lats,),
        in_specs=[
            pl.BlockSpec(orders.shape, lambda i: (0,)),
            pl.BlockSpec((levels, 1, times, lon_count), lambda i: (0, i, 0, 0)),
        ],
        out_specs=pl.BlockSpec((levels, bands, 1, pairs, 8, 128), lambda i: (0, 0, i, 0, 0, 0)),
        out_shape=jax.ShapeDtypeStruct((levels, bands, lats, pairs, 8, 128), BF16),
        scratch_shapes=[pltpu.VMEM((rows, 128), F32), pltpu.VMEM((rows, lon_count), BF16)],
        cost_estimate=pl.CostEstimate(
            flops=2 * rows * levels * lats * times * lon_count,
            bytes_accessed=2 * levels * lats * times * (lon_count + rows),
            transcendentals=0,
        ),
        name="fourier",
    )(orders, fields)


def legendre_kernel(later, last, spectra_ref, basis_ref, *refs):
    if later:
        before_ref, refs = refs[1], refs[2:]
    part_ref, out_ref, wide_ref, side_ref, gram_ref, cross_ref = refs
    step = pl.program_id(0)

    @pl.when(step == 0)
    def _():
        gram_ref[...] = before_ref[...] if later else jnp.zeros_like(gram_ref)
        cross_ref[...] = jnp.zeros_like(cross_ref)

    lats = spectra_ref.shape[0]
    wide_ref[...] = spectra_ref[:, 0].astype(F32).reshape(lats * 8, 128)
    for half in range(2):
        for h in range(2):
            for c in range(2):
                piece = wide_ref[pl.ds(half * 4 + h * 2 + c, lats, stride=8), :]
                at = c * 256 + half * 128
                side_ref[h * lats:(h + 1) * lats, at:at + 128] = piece.astype(BF16)
    product = jnp.dot(basis_ref[0], side_ref[...], preferred_element_type=F32)
    flip = (((0,), (0,)), ((), ()))
    for c in range(2):
        value = product[:, c * 256:(c + 1) * 256]
        high = value.astype(BF16)
        low = (value - high.astype(F32)).astype(BF16)
        part_ref[0, c, :, :256] = high
        part_ref[0, c, :, 256:] = low
        gram_ref[...] += lax.dot_general(high, high, flip, preferred_element_type=F32)
        gram_ref[...] += lax.dot_general(low, low, flip, preferred_element_type=F32)
        cross_ref[...] += lax.dot_general(high, low, flip, preferred_element_type=F32)

    @pl.when(step == pl.num_programs(0) - 1)
    def _():
        total = gram_ref[...] + cross_ref[...] + cross_ref[...].T
        if last:
            out_ref[...] = jnp.stack([total[:, :128], total[:, 128:]]).reshape(out_ref.shape)
        else:
            out_ref[...] = total


def project(spectra, legendre, start, carried, last):
    lats, pairs = spectra.shape[:2]
    pairs_total, rows, both = legendre.shape
    whole = pl.BlockSpec((256, 256), lambda q: (0, 0))
    later = carried is not None
    pieces = (128, 4, 128) if last else (256, 256)
    return pl.pallas_call(
        functools.partial(legendre_kernel, later, last),
        grid=(pairs,),
        in_specs=[
            pl.BlockSpec((lats, 1, 8, 128), lambda q: (0, q, 0, 0)),
            pl.BlockSpec((1, rows, both), lambda q: (q + start, 0, 0)),
        ] + ([pl.BlockSpec(memory_space=pl.ANY), whole] if later else []),
        out_specs=[
            pl.BlockSpec((1, 2, rows, 512), lambda q: (q + start, 0, 0, 0)),
            pl.BlockSpec(pieces, lambda q: (0,) * len(pieces)),
        ],
        out_shape=[
            jax.ShapeDtypeStruct((pairs_total, 2, rows, 512), BF16),
            jax.ShapeDtypeStruct(pieces, F32),
        ],
        scratch_shapes=[
            pltpu.VMEM((lats * 8, 128), F32),
            pltpu.VMEM((both, 512), BF16),
            pltpu.VMEM((256, 256), F32),
            pltpu.VMEM((256, 256), F32),
        ],
        input_output_aliases={2: 0} if later else {},
        cost_estimate=pl.CostEstimate(
            flops=pairs * (2 * rows * both * 512 + 12 * rows * 256 * 256),
            bytes_accessed=pairs * (lats * 2048 + 2 * rows * both + rows * 2048),
            transcendentals=0,
        ),
        name="legendre",
    )(spectra, legendre, *(carried or ()))


def factor_block(groups, width):
    count = len(groups)
    n = count * 8
    shape = (8, n)
    lane = lax.broadcasted_iota(jnp.int32, shape, 1)
    sub = lax.broadcasted_iota(jnp.int32, shape, 0)
    work = list(groups)
    upper, inverse = [jnp.zeros(shape, F32)] * count, [jnp.zeros(shape, F32)] * count
    for j in range(0, n, width):
        g, r = divmod(j, 8)
        inside = (lane >= j) & (lane < j + width)
        cols = [
            [jnp.broadcast_to(work[k][:, j + a:j + a + 1], shape) for a in range(width)] for k in range(g, count)
        ]
        unit, plain, pivot, over, ratio = [], [], [], [], {}
        entry = {
            (b, a): jnp.broadcast_to(cols[0][a][r + b:r + b + 1], shape) for a in range(width) for b in range(a, width)
        }
        for a in range(width):
            pivot.append(entry[a, a])
            over.append(1.0 / pivot[a])
            for b in range(a + 1, width):
                ratio[b, a] = entry[b, a] * over[a]
            for b in range(a + 1, width):
                for e in range(b, width):
                    entry[e, b] = entry[e, b] - ratio[e, a] * entry[b, a]
        for a in range(width):
            row = jnp.broadcast_to(work[g][r + a:r + a + 1], shape)
            start = jnp.where(inside, jnp.where(lane == j + a, 1.0, 0.0), row)
            for b in range(a):
                row = row - ratio[a, b] * plain[b]
                start = start - ratio[a, b] * unit[b]
            plain.append(row)
            unit.append(start)
        down = [unit[a] * over[a] for a in range(width)]
        for k in range(g, count):
            if k == g and r + width == 8:
                continue
            moved = jnp.where(inside, 0.0, work[k])
            reduced = []
            for a in range(width):
                value = cols[k - g][a]
                for b in range(a):
                    value = value - ratio[a, b] * reduced[b]
                reduced.append(value)
                moved = moved - value * down[a]
            work[k] = moved if k > g else jnp.where(sub >= r + width, moved, work[k])
        for a in range(width):
            root = lax.rsqrt(pivot[a])
            up = jnp.where(lane >= j + a, plain[a], 0.0) * root
            inv = jnp.where(lane <= j + a, unit[a], 0.0) * root
            upper[g] = jnp.where(sub == r + a, up, upper[g])
            inverse[g] = jnp.where(sub == r + a, inv, inverse[g])
    return jnp.concatenate(upper, 0), jnp.concatenate(inverse, 0)


def f32_dot(a, b, dims=(((1,), (0,)), ((), ()))):
    return lax.dot_general(a, b, dims, precision=lax.Precision.HIGHEST, preferred_element_type=F32)


def factor_into(scale, gram_ref, factor_ref, inverse_ref, block_ref):
    half = gram_ref.shape[0] // 2
    flip = (((0,), (0,)), ((), ()))
    block_ref[...] = gram_ref[:half, :half] * scale

    def step(index, carry):
        upper, inverse = factor_block([block_ref[k * 8:(k + 1) * 8, :] for k in range(half // 8)], 8)

        @pl.when(index == 0)
        def _():
            factor_ref[:half, :half] = upper
            inverse_ref[:half, :half] = inverse
            side = f32_dot(inverse, gram_ref[:half, half:] * scale)
            factor_ref[:half, half:] = side
            block_ref[...] = gram_ref[half:, half:] * scale - f32_dot(side, side, flip)

        @pl.when(index == 1)
        def _():
            factor_ref[half:, half:] = upper
            inverse_ref[half:, half:] = inverse
            below = f32_dot(factor_ref[:half, half:], inverse_ref[:half, :half], flip)
            inverse_ref[half:, :half] = -f32_dot(inverse, below)

        return carry

    lax.fori_loop(0, 2, step, 0)
    factor_ref[half:, :half] = jnp.zeros((half, half), F32)
    inverse_ref[:half, half:] = jnp.zeros((half, half), F32)


def finish_kernel(
    scale, pieces_ref, part_any, out_ref, factor_ref, gram_ref, inverse_ref, block_ref, weight_ref, part_ref, sems
):
    pair = pl.program_id(0)

    def fetch(index):
        return pltpu.make_async_copy(part_any.at[index], part_ref.at[index], sems.at[index])

    @pl.when(pair == 0)
    def _():
        for index in range(part_ref.shape[0]):
            fetch(index).start()
        gram_ref[:, :128] = pieces_ref[:64].reshape(256, 128)
        gram_ref[:, 128:] = pieces_ref[64:].reshape(256, 128)
        factor_into(scale, gram_ref, factor_ref, inverse_ref, block_ref)
        turned = inverse_ref[...].T
        top = turned.astype(BF16)
        weight_ref[:256] = top
        weight_ref[256:512] = top
        weight_ref[512:] = (turned - top.astype(F32)).astype(BF16)

    fetch(pair).wait()
    for c in range(2):
        part = part_ref[pair, c]
        wide = jnp.concatenate([part, part[:, :256]], axis=1)
        value = jnp.dot(wide, weight_ref[...], preferred_element_type=F32)
        out_ref[0, :, c, :] = value.astype(BF16)


def finish(pieces, parts, total_rows):
    pairs, _, degree_rows, _ = parts.shape
    return pl.pallas_call(
        functools.partial(finish_kernel, 1.0 / total_rows),
        grid=(pairs,),
        in_specs=[pl.BlockSpec(pieces.shape, lambda q: (0, 0, 0)), pl.BlockSpec(memory_space=pl.ANY)],
        out_specs=[
            pl.BlockSpec((1, degree_rows, 2, 256), lambda q: (q, 0, 0, 0)),
            pl.BlockSpec((256, 256), lambda q: (0, 0)),
        ],
        out_shape=[
            jax.ShapeDtypeStruct((pairs, degree_rows, 2, 256), BF16),
            jax.ShapeDtypeStruct((256, 256), F32),
        ],
        scratch_shapes=[
            pltpu.VMEM((256, 256), F32),
            pltpu.VMEM((256, 256), F32),
            pltpu.VMEM((128, 128), F32),
            pltpu.VMEM((768, 256), BF16),
            pltpu.VMEM(parts.shape, BF16),
            pltpu.SemaphoreType.DMA((pairs,)),
        ],
        name="finish",
    )(pieces, parts)


def exchange(value):
    return lax.all_to_all(value, AXES, split_axis=0, concat_axis=0, tiled=True)


def reduce_gram(pieces):
    total = exchange(pieces).sum(axis=0, keepdims=True)
    return exchange(jnp.broadcast_to(total, pieces.shape))


def shards(fields, wave_order, basis):
    levels, times, lats, lon_count = fields.shape
    groups, bands = lax.axis_size("grp"), lax.axis_size("band")
    pairs, _, lat_total, degree_rows = basis.shape
    fields = fields.transpose(0, 2, 1, 3)
    orders = wave_order
    starts = [sum(CHUNKS[:n]) for n in range(len(CHUNKS))]
    received = []
    for chunk in zip(starts, CHUNKS):
        sent = transform(fields, orders, bands, pairs, chunk)
        received.append(exchange(sent.reshape(groups * bands, lats, chunk[1], 8, 128)))
    legendre = basis.transpose(0, 3, 1, 2).reshape(pairs, degree_rows, 2 * lat_total)
    carried = None
    for start, spectra in zip(starts, received):
        last = start == starts[-1]
        carried = project(spectra.reshape(lat_total, -1, 8, 128), legendre, start, carried, last)
    parts, pieces = carried
    whitened, factor = finish(reduce_gram(pieces), parts, levels * pairs * bands * 2 * degree_rows)
    return (whitened.transpose(0, 2, 1, 3)[None], factor)


def solution(mesh):
    placed = (P(None, None, ("grp", "band"), None), P(), P("band", None, None, None))
    return jax.shard_map(
        shards,
        mesh=mesh,
        in_specs=placed,
        out_specs=(P("grp", "band", None, None, None), P()),
        check_vma=False,
    )
```

```python
import functools
import math

import jax
import jax.numpy as jnp
from jax import lax
from jax.experimental import pallas as pl
from jax.experimental.pallas import tpu as pltpu
from jax.sharding import PartitionSpec as P

F32 = jnp.float32
BF16 = jnp.bfloat16
AXES = ("grp", "band")
CHUNKS = (1, 4)


def cos_sin_quarter(position, lon_count):
    quarter = lon_count / 4.0
    turn = jnp.floor((position + quarter / 2.0) * (1.0 / quarter))
    angle = (position - turn * quarter) * (2.0 * math.pi / lon_count)
    square = angle * angle
    cosine = 1.0 + square * (-0.5 + square * (1.0 / 24 + square * (-1.0 / 720 + square * (1.0 / 40320))))
    sine = angle * (1.0 + square * (-1.0 / 6 + square * (1.0 / 120 + square * (-1.0 / 5040 + square * (1.0 / 362880)))))
    odd = (turn == 1.0) | (turn == 3.0)
    first = jnp.where(odd, sine, cosine)
    second = jnp.where(odd, cosine, sine)
    first = jnp.where((turn == 1.0) | (turn == 2.0), -first, first)
    second = jnp.where((turn == 2.0) | (turn == 3.0), -second, second)
    return first, second


def wrap(value, period):
    return value - period * jnp.floor((value + 0.5) * (1.0 / period))


def build_table(chunk, pairs_total, orders_ref, wave_ref, table_ref, lon_count):
    start, pairs = chunk
    lanes = 128
    step_rows = 32
    half_blocks = lon_count // lanes // 2
    rows = table_ref.shape[0] // pairs
    orders = orders_ref[...].astype(F32).reshape(1, -1)
    high = jnp.floor((orders + 0.5) * (1.0 / 32))
    low = orders - 32.0 * high
    high = jnp.broadcast_to(high, (lanes, high.shape[1])).astype(BF16)
    low = jnp.broadcast_to(low, (lanes, low.shape[1])).astype(BF16)
    shape = (rows, orders.shape[1])
    row = lax.broadcasted_iota(jnp.int32, shape, 0)
    slot = lax.broadcasted_iota(jnp.int32, shape, 1)
    across = (((1,), (1,)), ((), ()))
    for pair in range(pairs):
        wanted = (row // 4) * (2 * pairs_total) + 2 * (start + pair) + (row // 2) % 2
        choice = jnp.where(slot == wanted, 1.0, 0.0).astype(BF16)
        wave_ref[pair * rows:(pair + 1) * rows, :] = 32.0 * lax.dot_general(
            choice, high, across, preferred_element_type=F32
        ) + lax.dot_general(choice, low, across, preferred_element_type=F32)

    def body(index, carry):
        at = pl.ds(pl.multiple_of(index * step_rows, step_rows), step_rows)
        wave = wave_ref[at, :]
        lane = lax.broadcasted_iota(jnp.int32, wave.shape, 1).astype(F32)
        parity = lax.broadcasted_iota(jnp.int32, wave.shape, 0) % 2
        quarter = jnp.where(parity == 1, lon_count / 4.0, 0.0)
        real, imag = cos_sin_quarter(wrap(wave * lane + quarter, float(lon_count)), lon_count)
        turn_real, turn_imag = cos_sin_quarter(wrap(wave * float(lanes), float(lon_count)), lon_count)
        sign = 1.0 - 2.0 * wrap(wave, 2.0)
        for block in range(half_blocks):
            table_ref[at, block * lanes:(block + 1) * lanes] = real.astype(BF16)
            other = block + half_blocks
            table_ref[at, other * lanes:(other + 1) * lanes] = (real * sign).astype(BF16)
            if block + 1 < half_blocks:
                real, imag = real * turn_real - imag * turn_imag, real * turn_imag + imag * turn_real
        return carry

    lax.fori_loop(0, table_ref.shape[0] // step_rows, body, 0)


def fourier_kernel(chunk, pairs_total, orders_ref, field_any, out_ref, wave_ref, table_ref, field_ref, sems):
    levels, lats, _, lon_count = field_ref.shape

    def fetch(lat):
        return pltpu.make_async_copy(field_any.at[:, lat], field_ref.at[:, lat], sems.at[lat])

    for lat in range(lats):
        fetch(lat).start()
    build_table(chunk, pairs_total, orders_ref, wave_ref, table_ref, lon_count)
    pairs = chunk[1]
    rows = table_ref.shape[0] // pairs

    def body(lat, carry):
        fetch(lat).wait()
        for level in range(levels):
            field = field_ref[level, lat]
            whole = lax.dot_general(table_ref[...], field, (((1,), (1,)), ((), ())), preferred_element_type=F32)
            for pair in range(pairs):
                result = whole[pair * rows:(pair + 1) * rows]
                left = result[:, :128].reshape(rows // 8, 8, 128)
                right = result[:, 128:].reshape(rows // 8, 8, 128)
                low = lax.broadcasted_iota(jnp.int32, left.shape, 1) < 4
                even = jnp.where(low, left, pltpu.roll(right, 4, 1))
                odd = jnp.where(low, pltpu.roll(left, 4, 1), right)
                mixed = jnp.stack([even, odd], axis=1).reshape(rows // 4, 8, 128)
                out_ref[level, :, lat, pair] = mixed.astype(BF16)
        return carry

    lax.fori_loop(0, lats, body, 0)


def transform(fields, orders, bands, pairs_total, chunk):
    levels, lats, times, lon_count = fields.shape
    pairs = chunk[1]
    rows = pairs * bands * 4
    near = pl.BlockSpec(memory_space=pltpu.VMEM)
    return pl.pallas_call(
        functools.partial(fourier_kernel, chunk, pairs_total),
        in_specs=[near, pl.BlockSpec(memory_space=pl.ANY)],
        out_specs=near,
        out_shape=jax.ShapeDtypeStruct((levels, bands, lats, pairs, 8, 128), BF16),
        scratch_shapes=[
            pltpu.VMEM((rows, 128), F32),
            pltpu.VMEM((rows, lon_count), BF16),
            pltpu.VMEM(fields.shape, BF16),
            pltpu.SemaphoreType.DMA((lats,)),
        ],
        cost_estimate=pl.CostEstimate(
            flops=2 * rows * levels * lats * times * lon_count,
            bytes_accessed=2 * levels * lats * times * (lon_count + rows),
            transcendentals=0,
        ),
        name="fourier",
    )(orders, fields)


def legendre_kernel(later, last, spectra_ref, basis_ref, *refs):
    if later:
        before_ref, refs = refs[1], refs[2:]
    part_ref, out_ref, wide_ref, side_ref, gram_ref, cross_ref = refs
    step = pl.program_id(0)

    @pl.when(step == 0)
    def _():
        gram_ref[...] = before_ref[...] if later else jnp.zeros_like(gram_ref)
        cross_ref[...] = jnp.zeros_like(cross_ref)

    lats = spectra_ref.shape[0]
    wide_ref[...] = spectra_ref[:, 0].astype(F32).reshape(lats * 8, 128)
    for half in range(2):
        for h in range(2):
            for c in range(2):
                piece = wide_ref[pl.ds(half * 4 + h * 2 + c, lats, stride=8), :]
                at = c * 256 + half * 128
                side_ref[h * lats:(h + 1) * lats, at:at + 128] = piece.astype(BF16)
    product = jnp.dot(basis_ref[0], side_ref[...], preferred_element_type=F32)
    flip = (((0,), (0,)), ((), ()))
    for c in range(2):
        value = product[:, c * 256:(c + 1) * 256]
        high = value.astype(BF16)
        low = (value - high.astype(F32)).astype(BF16)
        part_ref[0, c, :, :256] = high
        part_ref[0, c, :, 256:] = low
        gram_ref[...] += lax.dot_general(high, high, flip, preferred_element_type=F32)
        gram_ref[...] += lax.dot_general(low, low, flip, preferred_element_type=F32)
        cross_ref[...] += lax.dot_general(high, low, flip, preferred_element_type=F32)

    @pl.when(step == pl.num_programs(0) - 1)
    def _():
        total = gram_ref[...] + cross_ref[...] + cross_ref[...].T
        if last:
            out_ref[...] = jnp.stack([total[:, :128], total[:, 128:]]).reshape(out_ref.shape)
        else:
            out_ref[...] = total


def project(spectra, legendre, start, carried, last):
    lats, pairs = spectra.shape[:2]
    pairs_total, rows, both = legendre.shape
    whole = pl.BlockSpec((256, 256), lambda q: (0, 0))
    later = carried is not None
    pieces = (128, 4, 128) if last else (256, 256)
    return pl.pallas_call(
        functools.partial(legendre_kernel, later, last),
        grid=(pairs,),
        in_specs=[
            pl.BlockSpec((lats, 1, 8, 128), lambda q: (0, q, 0, 0)),
            pl.BlockSpec((1, rows, both), lambda q: (q + start, 0, 0)),
        ] + ([pl.BlockSpec(memory_space=pl.ANY), whole] if later else []),
        out_specs=[
            pl.BlockSpec((1, 2, rows, 512), lambda q: (q + start, 0, 0, 0)),
            pl.BlockSpec(pieces, lambda q: (0,) * len(pieces)),
        ],
        out_shape=[
            jax.ShapeDtypeStruct((pairs_total, 2, rows, 512), BF16),
            jax.ShapeDtypeStruct(pieces, F32),
        ],
        scratch_shapes=[
            pltpu.VMEM((lats * 8, 128), F32),
            pltpu.VMEM((both, 512), BF16),
            pltpu.VMEM((256, 256), F32),
            pltpu.VMEM((256, 256), F32),
        ],
        input_output_aliases={2: 0} if later else {},
        cost_estimate=pl.CostEstimate(
            flops=pairs * (2 * rows * both * 512 + 12 * rows * 256 * 256),
            bytes_accessed=pairs * (lats * 2048 + 2 * rows * both + rows * 2048),
            transcendentals=0,
        ),
        name="legendre",
    )(spectra, legendre, *(carried or ()))


def factor_block(groups, width):
    count = len(groups)
    n = count * 8
    shape = (8, n)
    lane = lax.broadcasted_iota(jnp.int32, shape, 1)
    sub = lax.broadcasted_iota(jnp.int32, shape, 0)
    work = list(groups)
    upper, inverse = [jnp.zeros(shape, F32)] * count, [jnp.zeros(shape, F32)] * count
    for j in range(0, n, width):
        g, r = divmod(j, 8)
        inside = (lane >= j) & (lane < j + width)
        cols = [
            [jnp.broadcast_to(work[k][:, j + a:j + a + 1], shape) for a in range(width)] for k in range(g, count)
        ]
        unit, plain, pivot, over, ratio = [], [], [], [], {}
        entry = {
            (b, a): jnp.broadcast_to(cols[0][a][r + b:r + b + 1], shape) for a in range(width) for b in range(a, width)
        }
        for a in range(width):
            pivot.append(entry[a, a])
            over.append(1.0 / pivot[a])
            for b in range(a + 1, width):
                ratio[b, a] = entry[b, a] * over[a]
            for b in range(a + 1, width):
                for e in range(b, width):
                    entry[e, b] = entry[e, b] - ratio[e, a] * entry[b, a]
        for a in range(width):
            row = jnp.broadcast_to(work[g][r + a:r + a + 1], shape)
            start = jnp.where(inside, jnp.where(lane == j + a, 1.0, 0.0), row)
            for b in range(a):
                row = row - ratio[a, b] * plain[b]
                start = start - ratio[a, b] * unit[b]
            plain.append(row)
            unit.append(start)
        down = [unit[a] * over[a] for a in range(width)]
        for k in range(g, count):
            if k == g and r + width == 8:
                continue
            moved = jnp.where(inside, 0.0, work[k])
            reduced = []
            for a in range(width):
                value = cols[k - g][a]
                for b in range(a):
                    value = value - ratio[a, b] * reduced[b]
                reduced.append(value)
                moved = moved - value * down[a]
            work[k] = moved if k > g else jnp.where(sub >= r + width, moved, work[k])
        for a in range(width):
            root = lax.rsqrt(pivot[a])
            up = jnp.where(lane >= j + a, plain[a], 0.0) * root
            inv = jnp.where(lane <= j + a, unit[a], 0.0) * root
            upper[g] = jnp.where(sub == r + a, up, upper[g])
            inverse[g] = jnp.where(sub == r + a, inv, inverse[g])
    return jnp.concatenate(upper, 0), jnp.concatenate(inverse, 0)


def f32_dot(a, b, dims=(((1,), (0,)), ((), ()))):
    return lax.dot_general(a, b, dims, precision=lax.Precision.HIGHEST, preferred_element_type=F32)


def factor_into(scale, gram_ref, factor_ref, inverse_ref, block_ref):
    half = gram_ref.shape[0] // 2
    flip = (((0,), (0,)), ((), ()))
    block_ref[...] = gram_ref[:half, :half] * scale

    def step(index, carry):
        upper, inverse = factor_block([block_ref[k * 8:(k + 1) * 8, :] for k in range(half // 8)], 8)

        @pl.when(index == 0)
        def _():
            factor_ref[:half, :half] = upper
            inverse_ref[:half, :half] = inverse
            side = f32_dot(inverse, gram_ref[:half, half:] * scale)
            factor_ref[:half, half:] = side
            block_ref[...] = gram_ref[half:, half:] * scale - f32_dot(side, side, flip)

        @pl.when(index == 1)
        def _():
            factor_ref[half:, half:] = upper
            inverse_ref[half:, half:] = inverse
            below = f32_dot(factor_ref[:half, half:], inverse_ref[:half, :half], flip)
            inverse_ref[half:, :half] = -f32_dot(inverse, below)

        return carry

    lax.fori_loop(0, 2, step, 0)
    factor_ref[half:, :half] = jnp.zeros((half, half), F32)
    inverse_ref[:half, half:] = jnp.zeros((half, half), F32)


def finish_kernel(
    scale, pieces_ref, part_any, out_ref, factor_ref, gram_ref, inverse_ref, block_ref, weight_ref, part_ref, sems
):
    pair = pl.program_id(0)

    def fetch(index):
        return pltpu.make_async_copy(part_any.at[index], part_ref.at[index], sems.at[index])

    @pl.when(pair == 0)
    def _():
        for index in range(part_ref.shape[0]):
            fetch(index).start()
        gram_ref[:, :128] = pieces_ref[:64].reshape(256, 128)
        gram_ref[:, 128:] = pieces_ref[64:].reshape(256, 128)
        factor_into(scale, gram_ref, factor_ref, inverse_ref, block_ref)
        turned = inverse_ref[...].T
        top = turned.astype(BF16)
        weight_ref[:256] = top
        weight_ref[256:512] = top
        weight_ref[512:] = (turned - top.astype(F32)).astype(BF16)

    fetch(pair).wait()
    for c in range(2):
        part = part_ref[pair, c]
        wide = jnp.concatenate([part, part[:, :256]], axis=1)
        value = jnp.dot(wide, weight_ref[...], preferred_element_type=F32)
        out_ref[0, :, c, :] = value.astype(BF16)


def finish(pieces, parts, total_rows):
    pairs, _, degree_rows, _ = parts.shape
    return pl.pallas_call(
        functools.partial(finish_kernel, 1.0 / total_rows),
        grid=(pairs,),
        in_specs=[pl.BlockSpec(pieces.shape, lambda q: (0, 0, 0)), pl.BlockSpec(memory_space=pl.ANY)],
        out_specs=[
            pl.BlockSpec((1, degree_rows, 2, 256), lambda q: (q, 0, 0, 0)),
            pl.BlockSpec((256, 256), lambda q: (0, 0)),
        ],
        out_shape=[
            jax.ShapeDtypeStruct((pairs, degree_rows, 2, 256), BF16),
            jax.ShapeDtypeStruct((256, 256), F32),
        ],
        scratch_shapes=[
            pltpu.VMEM((256, 256), F32),
            pltpu.VMEM((256, 256), F32),
            pltpu.VMEM((128, 128), F32),
            pltpu.VMEM((768, 256), BF16),
            pltpu.VMEM(parts.shape, BF16),
            pltpu.SemaphoreType.DMA((pairs,)),
        ],
        name="finish",
    )(pieces, parts)


def exchange(value):
    return lax.all_to_all(value, AXES, split_axis=0, concat_axis=0, tiled=True)


def reduce_gram(pieces):
    total = exchange(pieces).sum(axis=0, keepdims=True)
    return exchange(jnp.broadcast_to(total, pieces.shape))


def shards(fields, wave_order, basis):
    levels, times, lats, lon_count = fields.shape
    groups, bands = lax.axis_size("grp"), lax.axis_size("band")
    pairs, _, lat_total, degree_rows = basis.shape
    fields = fields.transpose(0, 2, 1, 3)
    orders = wave_order
    starts = [sum(CHUNKS[:n]) for n in range(len(CHUNKS))]
    received = []
    for chunk in zip(starts, CHUNKS):
        sent = transform(fields, orders, bands, pairs, chunk)
        received.append(exchange(sent.reshape(groups * bands, lats, chunk[1], 8, 128)))
    legendre = basis.transpose(0, 3, 1, 2).reshape(pairs, degree_rows, 2 * lat_total)
    carried = None
    for start, spectra in zip(starts, received):
        last = start == starts[-1]
        carried = project(spectra.reshape(lat_total, -1, 8, 128), legendre, start, carried, last)
    parts, pieces = carried
    whitened, factor = finish(reduce_gram(pieces), parts, levels * pairs * bands * 2 * degree_rows)
    return (whitened.transpose(0, 2, 1, 3)[None], factor)


def solution(mesh):
    placed = (P(None, None, ("grp", "band"), None), P(), P("band", None, None, None))
    return jax.shard_map(
        shards,
        mesh=mesh,
        in_specs=placed,
        out_specs=(P("grp", "band", None, None, None), P()),
        check_vma=False,
    )
```

```python
import functools
import math

import jax
import jax.numpy as jnp
from jax import lax
from jax.experimental import pallas as pl
from jax.experimental.pallas import tpu as pltpu
from jax.sharding import PartitionSpec as P

F32 = jnp.float32
BF16 = jnp.bfloat16
AXES = ("grp", "band")
CHUNKS = (2, 3)


def cos_sin_quarter(position, lon_count):
    quarter = lon_count / 4.0
    turn = jnp.floor((position + quarter / 2.0) * (1.0 / quarter))
    angle = (position - turn * quarter) * (2.0 * math.pi / lon_count)
    square = angle * angle
    cosine = 1.0 + square * (-0.5 + square * (1.0 / 24 + square * (-1.0 / 720 + square * (1.0 / 40320))))
    sine = angle * (1.0 + square * (-1.0 / 6 + square * (1.0 / 120 + square * (-1.0 / 5040 + square * (1.0 / 362880)))))
    odd = (turn == 1.0) | (turn == 3.0)
    first = jnp.where(odd, sine, cosine)
    second = jnp.where(odd, cosine, sine)
    first = jnp.where((turn == 1.0) | (turn == 2.0), -first, first)
    second = jnp.where((turn == 2.0) | (turn == 3.0), -second, second)
    return first, second


def wrap(value, period):
    return value - period * jnp.floor((value + 0.5) * (1.0 / period))


def build_table(chunk, pairs_total, orders_ref, wave_ref, table_ref, lon_count):
    start, pairs = chunk
    lanes = 128
    step_rows = 32
    half_blocks = lon_count // lanes // 2
    rows = table_ref.shape[0] // pairs
    orders = orders_ref[...].astype(F32).reshape(1, -1)
    high = jnp.floor((orders + 0.5) * (1.0 / 32))
    low = orders - 32.0 * high
    high = jnp.broadcast_to(high, (lanes, high.shape[1])).astype(BF16)
    low = jnp.broadcast_to(low, (lanes, low.shape[1])).astype(BF16)
    shape = (rows, orders.shape[1])
    row = lax.broadcasted_iota(jnp.int32, shape, 0)
    slot = lax.broadcasted_iota(jnp.int32, shape, 1)
    across = (((1,), (1,)), ((), ()))
    for pair in range(pairs):
        wanted = (row // 4) * (2 * pairs_total) + 2 * (start + pair) + (row // 2) % 2
        choice = jnp.where(slot == wanted, 1.0, 0.0).astype(BF16)
        wave_ref[pair * rows:(pair + 1) * rows, :] = 32.0 * lax.dot_general(
            choice, high, across, preferred_element_type=F32
        ) + lax.dot_general(choice, low, across, preferred_element_type=F32)

    def body(index, carry):
        at = pl.ds(pl.multiple_of(index * step_rows, step_rows), step_rows)
        wave = wave_ref[at, :]
        lane = lax.broadcasted_iota(jnp.int32, wave.shape, 1).astype(F32)
        parity = lax.broadcasted_iota(jnp.int32, wave.shape, 0) % 2
        quarter = jnp.where(parity == 1, lon_count / 4.0, 0.0)
        real, imag = cos_sin_quarter(wrap(wave * lane + quarter, float(lon_count)), lon_count)
        turn_real, turn_imag = cos_sin_quarter(wrap(wave * float(lanes), float(lon_count)), lon_count)
        sign = 1.0 - 2.0 * wrap(wave, 2.0)
        for block in range(half_blocks):
            table_ref[at, block * lanes:(block + 1) * lanes] = real.astype(BF16)
            other = block + half_blocks
            table_ref[at, other * lanes:(other + 1) * lanes] = (real * sign).astype(BF16)
            if block + 1 < half_blocks:
                real, imag = real * turn_real - imag * turn_imag, real * turn_imag + imag * turn_real
        return carry

    lax.fori_loop(0, table_ref.shape[0] // step_rows, body, 0)


def fourier_kernel(chunk, pairs_total, orders_ref, field_any, out_ref, wave_ref, table_ref, field_ref, sems):
    levels, lats, _, lon_count = field_ref.shape

    def fetch(lat):
        return pltpu.make_async_copy(field_any.at[:, lat], field_ref.at[:, lat], sems.at[lat])

    for lat in range(lats):
        fetch(lat).start()
    build_table(chunk, pairs_total, orders_ref, wave_ref, table_ref, lon_count)
    pairs = chunk[1]
    rows = table_ref.shape[0] // pairs

    def body(lat, carry):
        fetch(lat).wait()
        for level in range(levels):
            field = field_ref[level, lat]
            whole = lax.dot_general(table_ref[...], field, (((1,), (1,)), ((), ())), preferred_element_type=F32)
            for pair in range(pairs):
                result = whole[pair * rows:(pair + 1) * rows]
                left = result[:, :128].reshape(rows // 8, 8, 128)
                right = result[:, 128:].reshape(rows // 8, 8, 128)
                low = lax.broadcasted_iota(jnp.int32, left.shape, 1) < 4
                even = jnp.where(low, left, pltpu.roll(right, 4, 1))
                odd = jnp.where(low, pltpu.roll(left, 4, 1), right)
                mixed = jnp.stack([even, odd], axis=1).reshape(rows // 4, 8, 128)
                out_ref[level, :, lat, pair] = mixed.astype(BF16)
        return carry

    lax.fori_loop(0, lats, body, 0)


def transform(fields, orders, bands, pairs_total, chunk):
    levels, lats, times, lon_count = fields.shape
    pairs = chunk[1]
    rows = pairs * bands * 4
    near = pl.BlockSpec(memory_space=pltpu.VMEM)
    return pl.pallas_call(
        functools.partial(fourier_kernel, chunk, pairs_total),
        in_specs=[near, pl.BlockSpec(memory_space=pl.ANY)],
        out_specs=near,
        out_shape=jax.ShapeDtypeStruct((levels, bands, lats, pairs, 8, 128), BF16),
        scratch_shapes=[
            pltpu.VMEM((rows, 128), F32),
            pltpu.VMEM((rows, lon_count), BF16),
            pltpu.VMEM(fields.shape, BF16),
            pltpu.SemaphoreType.DMA((lats,)),
        ],
        cost_estimate=pl.CostEstimate(
            flops=2 * rows * levels * lats * times * lon_count,
            bytes_accessed=2 * levels * lats * times * (lon_count + rows),
            transcendentals=0,
        ),
        name="fourier",
    )(orders, fields)


def legendre_kernel(later, last, spectra_ref, basis_ref, *refs):
    if later:
        before_ref, refs = refs[1], refs[2:]
    part_ref, out_ref, wide_ref, side_ref, gram_ref, cross_ref = refs
    step = pl.program_id(0)

    @pl.when(step == 0)
    def _():
        gram_ref[...] = before_ref[...] if later else jnp.zeros_like(gram_ref)
        cross_ref[...] = jnp.zeros_like(cross_ref)

    lats = spectra_ref.shape[0]
    wide_ref[...] = spectra_ref[:, 0].astype(F32).reshape(lats * 8, 128)
    for half in range(2):
        for h in range(2):
            for c in range(2):
                piece = wide_ref[pl.ds(half * 4 + h * 2 + c, lats, stride=8), :]
                at = c * 256 + half * 128
                side_ref[h * lats:(h + 1) * lats, at:at + 128] = piece.astype(BF16)
    product = jnp.dot(basis_ref[0], side_ref[...], preferred_element_type=F32)
    flip = (((0,), (0,)), ((), ()))
    for c in range(2):
        value = product[:, c * 256:(c + 1) * 256]
        high = value.astype(BF16)
        low = (value - high.astype(F32)).astype(BF16)
        part_ref[0, c, :, :256] = high
        part_ref[0, c, :, 256:] = low
        gram_ref[...] += lax.dot_general(high, high, flip, preferred_element_type=F32)
        gram_ref[...] += lax.dot_general(low, low, flip, preferred_element_type=F32)
        cross_ref[...] += lax.dot_general(high, low, flip, preferred_element_type=F32)

    @pl.when(step == pl.num_programs(0) - 1)
    def _():
        total = gram_ref[...] + cross_ref[...] + cross_ref[...].T
        if last:
            out_ref[...] = jnp.stack([total[:, :128], total[:, 128:]]).reshape(out_ref.shape)
        else:
            out_ref[...] = total


def project(spectra, legendre, start, carried, last):
    lats, pairs = spectra.shape[:2]
    pairs_total, rows, both = legendre.shape
    whole = pl.BlockSpec((256, 256), lambda q: (0, 0))
    later = carried is not None
    pieces = (128, 4, 128) if last else (256, 256)
    return pl.pallas_call(
        functools.partial(legendre_kernel, later, last),
        grid=(pairs,),
        in_specs=[
            pl.BlockSpec((lats, 1, 8, 128), lambda q: (0, q, 0, 0)),
            pl.BlockSpec((1, rows, both), lambda q: (q + start, 0, 0)),
        ] + ([pl.BlockSpec(memory_space=pl.ANY), whole] if later else []),
        out_specs=[
            pl.BlockSpec((1, 2, rows, 512), lambda q: (q + start, 0, 0, 0)),
            pl.BlockSpec(pieces, lambda q: (0,) * len(pieces)),
        ],
        out_shape=[
            jax.ShapeDtypeStruct((pairs_total, 2, rows, 512), BF16),
            jax.ShapeDtypeStruct(pieces, F32),
        ],
        scratch_shapes=[
            pltpu.VMEM((lats * 8, 128), F32),
            pltpu.VMEM((both, 512), BF16),
            pltpu.VMEM((256, 256), F32),
            pltpu.VMEM((256, 256), F32),
        ],
        input_output_aliases={2: 0} if later else {},
        cost_estimate=pl.CostEstimate(
            flops=pairs * (2 * rows * both * 512 + 12 * rows * 256 * 256),
            bytes_accessed=pairs * (lats * 2048 + 2 * rows * both + rows * 2048),
            transcendentals=0,
        ),
        name="legendre",
    )(spectra, legendre, *(carried or ()))


def factor_block(groups, width):
    count = len(groups)
    n = count * 8
    shape = (8, n)
    lane = lax.broadcasted_iota(jnp.int32, shape, 1)
    sub = lax.broadcasted_iota(jnp.int32, shape, 0)
    work = list(groups)
    upper, inverse = [jnp.zeros(shape, F32)] * count, [jnp.zeros(shape, F32)] * count
    for j in range(0, n, width):
        g, r = divmod(j, 8)
        inside = (lane >= j) & (lane < j + width)
        cols = [
            [jnp.broadcast_to(work[k][:, j + a:j + a + 1], shape) for a in range(width)] for k in range(g, count)
        ]
        unit, plain, pivot, over, ratio = [], [], [], [], {}
        entry = {
            (b, a): jnp.broadcast_to(cols[0][a][r + b:r + b + 1], shape) for a in range(width) for b in range(a, width)
        }
        for a in range(width):
            pivot.append(entry[a, a])
            over.append(1.0 / pivot[a])
            for b in range(a + 1, width):
                ratio[b, a] = entry[b, a] * over[a]
            for b in range(a + 1, width):
                for e in range(b, width):
                    entry[e, b] = entry[e, b] - ratio[e, a] * entry[b, a]
        for a in range(width):
            row = jnp.broadcast_to(work[g][r + a:r + a + 1], shape)
            start = jnp.where(inside, jnp.where(lane == j + a, 1.0, 0.0), row)
            for b in range(a):
                row = row - ratio[a, b] * plain[b]
                start = start - ratio[a, b] * unit[b]
            plain.append(row)
            unit.append(start)
        down = [unit[a] * over[a] for a in range(width)]
        for k in range(g, count):
            if k == g and r + width == 8:
                continue
            moved = jnp.where(inside, 0.0, work[k])
            reduced = []
            for a in range(width):
                value = cols[k - g][a]
                for b in range(a):
                    value = value - ratio[a, b] * reduced[b]
                reduced.append(value)
                moved = moved - value * down[a]
            work[k] = moved if k > g else jnp.where(sub >= r + width, moved, work[k])
        for a in range(width):
            root = lax.rsqrt(pivot[a])
            up = jnp.where(lane >= j + a, plain[a], 0.0) * root
            inv = jnp.where(lane <= j + a, unit[a], 0.0) * root
            upper[g] = jnp.where(sub == r + a, up, upper[g])
            inverse[g] = jnp.where(sub == r + a, inv, inverse[g])
    return jnp.concatenate(upper, 0), jnp.concatenate(inverse, 0)


def f32_dot(a, b, dims=(((1,), (0,)), ((), ()))):
    return lax.dot_general(a, b, dims, precision=lax.Precision.HIGHEST, preferred_element_type=F32)


def factor_into(scale, gram_ref, factor_ref, inverse_ref, block_ref):
    half = gram_ref.shape[0] // 2
    flip = (((0,), (0,)), ((), ()))
    block_ref[...] = gram_ref[:half, :half] * scale

    def step(index, carry):
        upper, inverse = factor_block([block_ref[k * 8:(k + 1) * 8, :] for k in range(half // 8)], 8)

        @pl.when(index == 0)
        def _():
            factor_ref[:half, :half] = upper
            inverse_ref[:half, :half] = inverse
            side = f32_dot(inverse, gram_ref[:half, half:] * scale)
            factor_ref[:half, half:] = side
            block_ref[...] = gram_ref[half:, half:] * scale - f32_dot(side, side, flip)

        @pl.when(index == 1)
        def _():
            factor_ref[half:, half:] = upper
            inverse_ref[half:, half:] = inverse
            below = f32_dot(factor_ref[:half, half:], inverse_ref[:half, :half], flip)
            inverse_ref[half:, :half] = -f32_dot(inverse, below)

        return carry

    lax.fori_loop(0, 2, step, 0)
    factor_ref[half:, :half] = jnp.zeros((half, half), F32)
    inverse_ref[:half, half:] = jnp.zeros((half, half), F32)


def finish_kernel(
    scale, pieces_ref, part_any, out_ref, factor_ref, gram_ref, inverse_ref, block_ref, weight_ref, part_ref, sems
):
    pair = pl.program_id(0)

    def fetch(index):
        return pltpu.make_async_copy(part_any.at[index], part_ref.at[index], sems.at[index])

    @pl.when(pair == 0)
    def _():
        for index in range(part_ref.shape[0]):
            fetch(index).start()
        gram_ref[:, :128] = pieces_ref[:64].reshape(256, 128)
        gram_ref[:, 128:] = pieces_ref[64:].reshape(256, 128)
        factor_into(scale, gram_ref, factor_ref, inverse_ref, block_ref)
        turned = inverse_ref[...].T
        top = turned.astype(BF16)
        weight_ref[:256] = top
        weight_ref[256:512] = top
        weight_ref[512:] = (turned - top.astype(F32)).astype(BF16)

    fetch(pair).wait()
    for c in range(2):
        part = part_ref[pair, c]
        wide = jnp.concatenate([part, part[:, :256]], axis=1)
        value = jnp.dot(wide, weight_ref[...], preferred_element_type=F32)
        out_ref[0, :, c, :] = value.astype(BF16)


def finish(pieces, parts, total_rows):
    pairs, _, degree_rows, _ = parts.shape
    return pl.pallas_call(
        functools.partial(finish_kernel, 1.0 / total_rows),
        grid=(pairs,),
        in_specs=[pl.BlockSpec(pieces.shape, lambda q: (0, 0, 0)), pl.BlockSpec(memory_space=pl.ANY)],
        out_specs=[
            pl.BlockSpec((1, degree_rows, 2, 256), lambda q: (q, 0, 0, 0)),
            pl.BlockSpec((256, 256), lambda q: (0, 0)),
        ],
        out_shape=[
            jax.ShapeDtypeStruct((pairs, degree_rows, 2, 256), BF16),
            jax.ShapeDtypeStruct((256, 256), F32),
        ],
        scratch_shapes=[
            pltpu.VMEM((256, 256), F32),
            pltpu.VMEM((256, 256), F32),
            pltpu.VMEM((128, 128), F32),
            pltpu.VMEM((768, 256), BF16),
            pltpu.VMEM(parts.shape, BF16),
            pltpu.SemaphoreType.DMA((pairs,)),
        ],
        name="finish",
    )(pieces, parts)


def exchange(value):
    return lax.all_to_all(value, AXES, split_axis=0, concat_axis=0, tiled=True)


def reduce_gram(pieces):
    total = exchange(pieces).sum(axis=0, keepdims=True)
    return exchange(jnp.broadcast_to(total, pieces.shape))


def shards(fields, wave_order, basis):
    levels, times, lats, lon_count = fields.shape
    groups, bands = lax.axis_size("grp"), lax.axis_size("band")
    pairs, _, lat_total, degree_rows = basis.shape
    fields = fields.transpose(0, 2, 1, 3)
    orders = wave_order
    starts = [sum(CHUNKS[:n]) for n in range(len(CHUNKS))]
    received = []
    for chunk in zip(starts, CHUNKS):
        sent = transform(fields, orders, bands, pairs, chunk)
        received.append(exchange(sent.reshape(groups * bands, lats, chunk[1], 8, 128)))
    legendre = basis.transpose(0, 3, 1, 2).reshape(pairs, degree_rows, 2 * lat_total)
    carried = None
    for start, spectra in zip(starts, received):
        last = start == starts[-1]
        carried = project(spectra.reshape(lat_total, -1, 8, 128), legendre, start, carried, last)
    parts, pieces = carried
    whitened, factor = finish(reduce_gram(pieces), parts, levels * pairs * bands * 2 * degree_rows)
    return (whitened.transpose(0, 2, 1, 3)[None], factor)


def solution(mesh):
    placed = (P(None, None, ("grp", "band"), None), P(), P("band", None, None, None))
    return jax.shard_map(
        shards,
        mesh=mesh,
        in_specs=placed,
        out_specs=(P("grp", "band", None, None, None), P()),
        check_vma=False,
    )
```
